32 devices in a mesh: groups: 2 (over x), frame: 8 (over z, y), chan: 2 (over core).
Axes of the slice: x: 2, y: 2, z: 4, core: 2. Of those that a mesh axis runs over, the one named last changes fastest.
Arguments:
- frames: bfloat16 [32, 64, 128, 128], P(('groups', 'frame'), 'chan'), parts along dimension 0, may hold values from -6 to 6
- spatial_weight: bfloat16 [9, 64, 64], replicated, may hold values from -0.25 to 0.25
- spatial_bias: float32 [64], replicated, may hold values from -3 to 3
- temporal_weight: bfloat16 [3, 64, 64], replicated, may hold values from -0.4375 to 0.4375
- cotangent: bfloat16 [32, 64, 16384], P('groups', None, ('frame', 'chan')), parts along dimension 0, may hold values from -6 to 6
Outputs:
- output: bfloat16 [32, 64, 16384], P('groups', None, ('frame', 'chan')), parts along dimension 0
- grad_spatial: float32 [18, 64, 64], P('groups'), parts along dimension 0
- grad_bias: float32 [128], P('groups'), parts along dimension 0
- grad_temporal: float32 [6, 64, 64], P('groups'), parts along dimension 0
The draws below stay inside these ranges and needn't reach their ends.
There are 2 independent parts, one for each index of `groups`. The reference program is written for one: setup_inputs(seed, part) draws one part's arguments, and reference() takes and returns one part's arrays. A program takes and returns all parts, laid end to end along the dimension named above; an argument that names none is the same for every part. Nothing has to cross between parts.
All inputs are finite; a program needn't handle non-finite values.
Results may differ from the reference program's by a relative error of at most 0.0055.
Values may be sent and summed in bfloat16 or wider, within the bound.
No kernel may reach another device: no remote copies, remote signals or barrier semaphores. Data moves between devices by JAX's collectives and lax.ppermute only.
A program may use at most 192 MiB of HBM per device.

```python
import jax
import jax.numpy as jnp
from jax import lax

C = 64
TAPS = 3
ROWS = 128
COLS = 128
FRAME_DILATION = 2
FRAMES = 16
PIX = 16384


def level_of(key, dims, shards, least, largest):
    gain, own = 1.0, jax.random.fold_in(key, 6)
    for position, parts in shards:
        draws = jnp.exp(jax.random.uniform(jax.random.fold_in(own, position), (parts,), jnp.float32, least / len(shards), largest / len(shards)))
        gain = gain * jnp.repeat(draws, dims[position] // parts).reshape([-1 if axis == position else 1 for axis in range(len(dims))])
    return gain


def centred(own_key, shape, width, bound, split=(), held_as=jnp.bfloat16):
    values = width * jax.random.normal(own_key, shape, jnp.float32)
    if split:
        values = values * level_of(own_key, shape, split, -0.22, 0.18)
    return jnp.clip(values, -bound, bound).astype(held_as)


def setup_inputs(seed: int = 0, part: int = 0) -> dict:
    arg_keys = jax.random.split(jax.random.key(seed), 6)
    own_keys = jax.random.split(jax.random.fold_in(arg_keys[5], part), 6)
    frames = centred(own_keys[0], (FRAMES, C, ROWS, COLS), 1.0, 6.0, ((0, 8), (1, 2)))
    spatial_weight = centred(arg_keys[1], (9, C, C), (9 * C) ** -0.5, 0.25)
    spatial_bias = centred(arg_keys[2], (C,), 0.5, 3.0, (), jnp.float32)
    temporal_weight = centred(arg_keys[3], (TAPS, C, C), (TAPS * C) ** -0.5, 0.4375)
    cotangent = centred(own_keys[4], (FRAMES, C, PIX), 1.0, 6.0, ((2, 16),))
    return dict(frames=frames, spatial_weight=spatial_weight, spatial_bias=spatial_bias, temporal_weight=temporal_weight, cotangent=cotangent)


def gelu_tanh(values):
    return 0.5 * values * (1.0 + jnp.tanh(0.7978845608 * (values + 0.044715 * values * values * values)))

def backward_delay(field, steps):
    if steps == 0:
        return field
    blank = jnp.zeros((steps,) + field.shape[1:], field.dtype)
    return jnp.concatenate([blank, field[:field.shape[0] - steps]], axis=0)

def forward_delay(field, steps):
    if steps == 0:
        return field
    blank = jnp.zeros((steps,) + field.shape[1:], field.dtype)
    return jnp.concatenate([field[steps:], blank], axis=0)

def reference(frames, spatial_weight, spatial_bias, temporal_weight, cotangent):
    total = frames.shape[0]
    padded = jnp.pad(frames.astype(jnp.float32), ((0, 0), (0, 0), (1, 1), (1, 1)))
    weights = spatial_weight.astype(jnp.float32)
    preact = jnp.zeros((total, C, ROWS, COLS), jnp.float32)
    for row_step in range(3):
        for col_step in range(3):
            window = padded[:, :, row_step:row_step + ROWS, col_step:col_step + COLS]
            preact = preact + jnp.einsum('oi,firc->forc', weights[3 * row_step + col_step], window)
    preact = preact + spatial_bias[None, :, None, None]
    activated, gelu_back = jax.vjp(gelu_tanh, preact)
    hidden_state = activated.astype(jnp.bfloat16).reshape(total, C, PIX).astype(jnp.float32)
    filter_weight = temporal_weight.astype(jnp.float32)
    input_gradients = cotangent.astype(jnp.float32)
    summed = hidden_state
    hidden_gradient = input_gradients
    temporal_grads = []
    for delay_index in range(TAPS):
        delayed_frames = backward_delay(hidden_state, delay_index * FRAME_DILATION)
        summed = summed + jnp.einsum('oi,tip->top', filter_weight[delay_index], delayed_frames)
        temporal_grads.append(jnp.einsum('top,tip->oi', input_gradients, delayed_frames))
        hidden_gradient = hidden_gradient + jnp.einsum('vn,cvb->cnb', filter_weight[delay_index], forward_delay(input_gradients, delay_index * FRAME_DILATION))
    output = summed.astype(jnp.bfloat16)
    grad_temporal = jnp.stack(temporal_grads)
    hidden_gradient = hidden_gradient.astype(jnp.bfloat16).reshape(total, C, ROWS, COLS).astype(jnp.float32)
    grad_preact = gelu_back(hidden_gradient)[0].astype(jnp.bfloat16).astype(jnp.float32)
    spatial_grads = []
    for row_step in range(3):
        for col_step in range(3):
            window = padded[:, :, row_step:row_step + ROWS, col_step:col_step + COLS]
            spatial_grads.append(jnp.einsum('forc,firc->oi', grad_preact, window))
    grad_spatial = jnp.stack(spatial_grads)
    grad_bias = lax.optimization_barrier(jnp.sum(grad_preact, axis=(0, 2, 3)))
    return (output, grad_spatial, grad_bias, grad_temporal)
```

```python
import jax
import jax.numpy as jnp
from jax import lax
from jax.experimental import pallas as pl
from jax.experimental.pallas import tpu as pltpu
from jax.sharding import PartitionSpec as P

FRAME_DILATION = 2
BOTH = ("frame", "chan")
F32 = jnp.float32
BF16 = jnp.bfloat16


def window_kernel(rows, images_ref, out_ref):
    block = pl.program_id(0)
    height = images_ref.shape[0]
    for step in range(rows + 2):
        row = block * rows + step - 1
        line = images_ref[jnp.clip(row, 0, height - 1)]
        if step == 0 or step == rows + 1:
            inside = jnp.logical_and(row >= 0, row < height)
            line = jnp.where(inside, line, jnp.zeros_like(line))
        out_ref[0, step] = line


def row_windows(images, blocks):
    height = images.shape[0]
    rows = height // blocks
    rest = images.shape[1:]
    zeros = (0,) * len(rest)
    return pl.pallas_call(
        lambda images_ref, out_ref: window_kernel(rows, images_ref, out_ref),
        out_shape=jax.ShapeDtypeStruct((blocks, rows + 2) + rest, images.dtype),
        grid=(blocks,),
        in_specs=[pl.BlockSpec(images.shape, lambda d: (0,) + zeros)],
        out_specs=pl.BlockSpec((1, rows + 2) + rest, lambda d: (d, 0) + zeros),
        name="row_windows",
    )(images)


def gelu_and_slope(values):
    square = values * values
    inner = 0.7978845608 * (values + 0.044715 * (square * values))
    bent = jnp.tanh(inner)
    half = 0.5 * (1.0 + bent)
    slope = half + (0.5 * values) * (1.0 - bent * bent) * (
        0.7978845608 + (3.0 * 0.044715 * 0.7978845608) * square
    )
    return half * values, slope


def layer_kernel(
    taps,
    side_ref,
    x_ref,
    cot_ref,
    sw_ref,
    bias_ref,
    tw_ref,
    out_ref,
    mine_ref,
    other_ref,
    cot_s,
    hid_s,
    w_s,
    ahead_s,
    back_s,
    bias_s,
    gp_s,
    gs_s,
    gt_s,
    gb_s,
    pack_s,
):
    step = pl.program_id(0)
    frames_in_all, channels, pixels = cot_ref.shape
    _, members, window_rows, local, width, cols = x_ref.shape
    rows = window_rows - 2
    lag = FRAME_DILATION
    margin = lag * (taps - 1)

    @pl.when(step == 0)
    def _():
        hid_s[pl.ds(0, margin)] = jnp.zeros((margin, channels, pixels), BF16)
        cot_s[pl.ds(frames_in_all, margin)] = jnp.zeros((margin, channels, pixels), BF16)
        cot_s[pl.ds(0, frames_in_all)] = cot_ref[...]
        for q in range(3):
            for s in range(3):
                w_s[s * channels : (s + 1) * channels, q * channels : (q + 1) * channels] = sw_ref[
                    3 * q + s
                ]
        for k in range(taps):
            ahead_s[:, k * channels : (k + 1) * channels] = jnp.transpose(
                tw_ref[k].astype(F32)
            ).astype(BF16)
            back_s[:, k * channels : (k + 1) * channels] = tw_ref[k]
        bias_s[...] = jnp.transpose(jnp.broadcast_to(bias_ref[...], (cols, channels)))
        gs_s[...] = jnp.zeros_like(gs_s)
        gt_s[...] = jnp.zeros_like(gt_s)
        gb_s[...] = jnp.zeros_like(gb_s)

    lane = lax.broadcasted_iota(jnp.int32, (channels, cols), 1)
    first = lane == 0
    last = lane == cols - 1
    chunk = 2 if rows % 2 == 0 else 1
    wide = chunk * cols

    def shifted(tile, by):
        if by == 1:
            return jnp.where(first, 0.0, pltpu.roll(tile, 1, 1))
        return jnp.where(last, 0.0, pltpu.roll(tile, cols - 1, 1))

    for j in range(local):
        t = step * local + j
        bias = bias_s[...]

        def stack_of(r):
            parts = []
            for q in range(3):
                for c in range(members):
                    parts.append(x_ref[0, c, r + q, j])
            return jnp.concatenate(parts, axis=0)

        for n in range(rows // chunk):
            at = n * wide
            stack = jnp.concatenate([stack_of(n * chunk + u) for u in range(chunk)], axis=1)
            conv = jnp.dot(w_s[...], stack, preferred_element_type=F32)
            ahead = jnp.concatenate(
                [cot_s[t + k * lag, :, at : at + wide] for k in range(taps)], axis=0
            )
            back_grad = jnp.dot(ahead_s[...], ahead, preferred_element_type=F32)
            back_grad = back_grad + cot_s[t, :, at : at + wide].astype(F32)
            back_grad = back_grad.astype(BF16).astype(F32)
            for u in range(chunk):
                lo = u * cols
                pre = (
                    shifted(conv[:channels, lo : lo + cols], 1)
                    + conv[channels : 2 * channels, lo : lo + cols]
                    + shifted(conv[2 * channels :, lo : lo + cols], -1)
                    + bias
                )
                hidden, slope = gelu_and_slope(pre)
                hid_s[t + margin, :, at + lo : at + lo + cols] = hidden.astype(BF16)
                rounded = (back_grad[:, lo : lo + cols] * slope).astype(BF16)
                grad = rounded.astype(F32)
                gb_s[...] += grad
                gp_s[0:channels, at + lo : at + lo + cols] = shifted(grad, -1).astype(BF16)
                gp_s[channels : 2 * channels, at + lo : at + lo + cols] = rounded
                gp_s[2 * channels :, at + lo : at + lo + cols] = shifted(grad, 1).astype(BF16)
            delayed = jnp.concatenate(
                [hid_s[t + margin - k * lag, :, at : at + wide] for k in range(taps)], axis=0
            )
            total = hid_s[t + margin, :, at : at + wide].astype(F32) + jnp.dot(
                back_s[...], delayed, preferred_element_type=F32
            )
            out_ref[j, :, at : at + wide] = total.astype(BF16)
        contract = (((1,), (1,)), ((), ()))
        whole = jnp.concatenate([stack_of(r) for r in range(rows)], axis=1)
        gs_s[...] += lax.dot_general(gp_s[...], whole, contract, preferred_element_type=F32)
        delayed = jnp.concatenate([hid_s[t + margin - k * lag] for k in range(taps)], axis=0)
        gt_s[...] += lax.dot_general(cot_s[t], delayed, contract, preferred_element_type=F32)

    @pl.when(step == pl.num_programs(0) - 1)
    def _():
        pieces = []
        for q in range(3):
            for s in range(3):
                pieces.append(
                    gs_s[s * channels : (s + 1) * channels, q * channels : (q + 1) * channels]
                )
        for k in range(taps):
            pieces.append(gt_s[:, k * channels : (k + 1) * channels])
        for p in range(len(pieces) // 2):
            pack_s[p * channels : (p + 1) * channels] = jnp.concatenate(
                pieces[2 * p : 2 * p + 2], axis=1
            )
        base = len(pieces) // 2 * channels
        sums = jnp.sum(jnp.transpose(gb_s[...]), axis=0, keepdims=True)
        pack_s[base:] = jnp.zeros((pack_s.shape[0] - base, 2 * channels), F32)
        pack_s[base : base + 1, 0:channels] = sums
        half = pack_s.shape[0] // 2
        side = side_ref[0]
        mine_ref[...] = pack_s[pl.ds(pl.multiple_of(side * half, 8), half)]
        other_ref[...] = pack_s[pl.ds(pl.multiple_of((1 - side) * half, 8), half)]


def run_layer(side, received, cotangent, spatial_weight, spatial_bias, temporal_weight):
    members = 2
    blocks, window_rows, local, width, cols = received.shape
    owners = blocks // members
    view = received.reshape(owners, members, window_rows, local, width, cols)
    total, channels, pixels = cotangent.shape
    taps = temporal_weight.shape[0]
    margin = FRAME_DILATION * (taps - 1)
    lines = (9 + taps + 1) // 2 * channels + 16
    half = lines // 2
    whole = lambda shape: pl.BlockSpec(shape, lambda i, s: (0,) * len(shape))
    return pl.pallas_call(
        lambda *refs: layer_kernel(taps, *refs),
        out_shape=(
            jax.ShapeDtypeStruct(cotangent.shape, BF16),
            jax.ShapeDtypeStruct((half, 2 * channels), F32),
            jax.ShapeDtypeStruct((half, 2 * channels), F32),
        ),
        grid_spec=pltpu.PrefetchScalarGridSpec(
            num_scalar_prefetch=1,
            grid=(owners,),
            in_specs=[
                pl.BlockSpec(
                    (1, members, window_rows, local, width, cols),
                    lambda i, s: (i, 0, 0, 0, 0, 0),
                ),
                whole(cotangent.shape),
                whole(spatial_weight.shape),
                whole((1, channels)),
                whole(temporal_weight.shape),
            ],
            out_specs=[
                pl.BlockSpec((local, channels, pixels), lambda i, s: (i, 0, 0)),
                whole((half, 2 * channels)),
                whole((half, 2 * channels)),
            ],
            scratch_shapes=[
                pltpu.VMEM((total + margin, channels, pixels), BF16),
                pltpu.VMEM((total + margin, channels, pixels), BF16),
                pltpu.VMEM((3 * channels, 3 * channels), BF16),
                pltpu.VMEM((channels, taps * channels), BF16),
                pltpu.VMEM((channels, taps * channels), BF16),
                pltpu.VMEM((channels, cols), F32),
                pltpu.VMEM((3 * channels, pixels), BF16),
                pltpu.VMEM((3 * channels, 3 * channels), F32),
                pltpu.VMEM((channels, taps * channels), F32),
                pltpu.VMEM((channels, cols), F32),
                pltpu.VMEM((lines, 2 * channels), F32),
            ],
        ),
        compiler_params=pltpu.CompilerParams(vmem_limit_bytes=48 << 20),
        name="layer",
    )(
        side,
        view,
        cotangent,
        spatial_weight,
        spatial_bias.reshape(1, channels),
        temporal_weight,
    )


def unpack_kernel(side_ref, mine_ref, other_ref, gs_ref, gb_ref, gt_ref, pack_s):
    half = mine_ref.shape[0]
    side = side_ref[0]
    pack_s[pl.ds(pl.multiple_of(side * half, 8), half)] = mine_ref[...]
    pack_s[pl.ds(pl.multiple_of((1 - side) * half, 8), half)] = other_ref[...]
    channels = gs_ref.shape[1]
    count = gs_ref.shape[0] + gt_ref.shape[0]
    for n in range(count):
        p, u = n // 2, n % 2
        piece = pack_s[p * channels : (p + 1) * channels, u * channels : (u + 1) * channels]
        if n < gs_ref.shape[0]:
            gs_ref[n] = piece
        else:
            gt_ref[n - gs_ref.shape[0]] = piece
    base = (count + 1) // 2 * channels
    gb_ref[...] = pack_s[base : base + 1, 0:channels]


def unpack(side, mine, other, taps, channels):
    half = mine.shape[0]
    return pl.pallas_call(
        unpack_kernel,
        out_shape=(
            jax.ShapeDtypeStruct((9, channels, channels), F32),
            jax.ShapeDtypeStruct((1, channels), F32),
            jax.ShapeDtypeStruct((taps, channels, channels), F32),
        ),
        in_specs=[
            pl.BlockSpec(memory_space=pltpu.SMEM),
            pl.BlockSpec((half, 2 * channels), lambda: (0, 0)),
            pl.BlockSpec((half, 2 * channels), lambda: (0, 0)),
        ],
        scratch_shapes=[pltpu.VMEM((2 * half, 2 * channels), F32)],
        name="unpack",
    )(side, mine, other)


def sum_over_devices(mine, other, owners):
    swap = [(0, 1), (1, 0)]
    part = mine + lax.ppermute(other, "chan", swap)
    bit = 1
    while bit < owners:
        part = part + lax.ppermute(part, "frame", [(i, i ^ bit) for i in range(owners)])
        bit *= 2
    return part, lax.ppermute(part, "chan", swap)


def make_body(owners, members):
    def body(frames, spatial_weight, spatial_bias, temporal_weight, cotangent):
        channels = spatial_weight.shape[1]
        taps = temporal_weight.shape[0]
        side = lax.axis_index("chan").astype(jnp.int32).reshape(1)
        images = jnp.transpose(frames, (2, 0, 1, 3))
        windows = row_windows(images, owners * members)
        received = lax.all_to_all(windows, BOTH, split_axis=0, concat_axis=0, tiled=True)
        output, mine, other = run_layer(
            side, received, cotangent, spatial_weight, spatial_bias, temporal_weight
        )
        part, rest = sum_over_devices(mine, other, owners)
        grad_spatial, grad_bias, grad_temporal = unpack(side, part, rest, taps, channels)
        return (output, grad_spatial, grad_bias.reshape(channels), grad_temporal)

    return body


def solution(mesh):
    return jax.shard_map(
        make_body(mesh.shape["frame"], mesh.shape["chan"]),
        mesh=mesh,
        in_specs=(
            P(("groups", "frame"), "chan", None, None),
            P(),
            P(),
            P(),
            P("groups", None, ("frame", "chan")),
        ),
        out_specs=(
            P("groups", None, ("frame", "chan")),
            P("groups", None, None),
            P("groups"),
            P("groups", None, None),
        ),
        check_vma=False,
    )
```

```python
import math

import jax
import jax.numpy as jnp
from jax import lax
from jax.experimental import pallas as pl
from jax.experimental.pallas import tpu as pltpu
from jax.sharding import PartitionSpec as P

FRAME_DILATION = 2
BOTH = ("frame", "chan")
F32 = jnp.float32
BF16 = jnp.bfloat16
LANES_IN_LANES = (((1,), (1,)), ((), ()))


def call(
    kernel, name, out_shape, flops, scratch=(), grid=None, in_specs=None, out_specs=None, **more
):
    shapes = out_shape if isinstance(out_shape, tuple) else (out_shape,)
    nbytes = sum(2 * math.prod(s.shape) * jnp.dtype(s.dtype).itemsize for s in shapes)
    cost = pl.CostEstimate(flops=flops, transcendentals=0, bytes_accessed=nbytes)
    params = dict(out_shape=out_shape, scratch_shapes=list(scratch), name=name, **more)
    params.update(cost_estimate=cost)
    if grid is not None:
        params.update(grid=grid)
    if in_specs is not None:
        params.update(in_specs=in_specs)
    if out_specs is not None:
        params.update(out_specs=out_specs)
    return pl.pallas_call(
        kernel, compiler_params=pltpu.CompilerParams(vmem_limit_bytes=24 << 20), **params
    )


IN_HBM = pl.BlockSpec(memory_space=pltpu.HBM)
ON_CHIP = pl.BlockSpec(memory_space=pltpu.VMEM)
SCALARS = pl.BlockSpec(memory_space=pltpu.SMEM)


def pack(frames, blocks):
    local, width, height, cols = frames.shape
    rows = height // blocks
    tile = min(height, 64)
    per = tile // rows

    def kernel(images_ref, out_ref):
        for j in range(local):
            lines = jnp.swapaxes(images_ref[j], 0, 1)
            for d in range(per):
                out_ref[d, j] = lines[d * rows : (d + 1) * rows]

    return call(
        kernel,
        "pack",
        pltpu.HBM((blocks, local, rows, width, cols), frames.dtype),
        frames.size,
        grid=(height // tile,),
        in_specs=[pl.BlockSpec((local, width, tile, cols), lambda i: (0, 0, i, 0))],
        out_specs=pl.BlockSpec((per, local, rows, width, cols), lambda i: (i, 0, 0, 0, 0)),
    )(pltpu.with_memory_space_constraint(frames, pltpu.HBM))


def edge_rows(side, lines):
    owners, members, local, rows, width, cols = lines.shape
    shape = jax.ShapeDtypeStruct((owners, members, local, width, cols), lines.dtype)

    def kernel(side_ref, lines_ref, near_ref, far_ref):
        @pl.when(side_ref[0] == 0)
        def _():
            near_ref[...] = lines_ref[:, :, :, rows - 1]
            far_ref[...] = lines_ref[:, :, :, 0]

        @pl.when(side_ref[0] == 1)
        def _():
            near_ref[...] = lines_ref[:, :, :, 0]
            far_ref[...] = lines_ref[:, :, :, rows - 1]

    return call(
        kernel,
        "edge_rows",
        (shape, shape),
        lines.size,
        in_specs=[SCALARS, ON_CHIP],
        out_specs=(ON_CHIP, ON_CHIP),
    )(side, lines)


def prepare(cotangent, temporal_weight, spatial_weight, bias, cols):
    total, channels, pixels = cotangent.shape
    taps = temporal_weight.shape[0]
    lag = FRAME_DILATION
    span = min(pixels, 256)

    def kernel(cot_ref, tw_ref, sw_ref, bias_ref, out_ref, w_ref, tile_ref, ahead_s):
        for k in range(taps):
            turned = jnp.transpose(tw_ref[k].astype(F32))
            ahead_s[:, k * channels : (k + 1) * channels] = turned.astype(BF16)
        for q in range(3):
            for s in range(3):
                w_ref[s * channels : (s + 1) * channels, q * channels : (q + 1) * channels] = (
                    sw_ref[3 * q + s]
                )
        tile_ref[...] = jnp.transpose(jnp.broadcast_to(bias_ref[...], (cols, channels)))
        for t in range(total):
            here = [k for k in range(taps) if t + k * lag < total]
            weights = ahead_s[:, : len(here) * channels]
            for at in range(0, pixels, span):
                ahead = jnp.concatenate(
                    [cot_ref[t + k * lag, :, at : at + span] for k in here], axis=0
                )
                grad = jnp.dot(weights, ahead, preferred_element_type=F32)
                grad = grad + cot_ref[t, :, at : at + span].astype(F32)
                out_ref[t, :, at : at + span] = grad.astype(BF16)

    return call(
        kernel,
        "prepare",
        (
            jax.ShapeDtypeStruct(cotangent.shape, BF16),
            jax.ShapeDtypeStruct((3 * channels, 3 * channels), BF16),
            jax.ShapeDtypeStruct((channels, cols), F32),
        ),
        8 * taps * channels * cotangent.size,
        scratch=[pltpu.VMEM((channels, taps * channels), BF16)],
        in_specs=[ON_CHIP] * 4,
        out_specs=(ON_CHIP,) * 3,
    )(cotangent, temporal_weight, spatial_weight, bias)


def temporal_output(inner, outer, temporal_weight, parity, rest=None):
    total, channels, inside = inner.shape
    span = outer.shape[2]
    cols = span // 2
    count = total // 2
    pixels = inside + span
    taps = temporal_weight.shape[0]

    def kernel(*refs):
        inner_ref, outer_ref, tw_ref, out_ref, w_s = refs[0], refs[1], refs[2], refs[-2], refs[-1]
        for k in range(taps):
            w_s[:, k * channels : (k + 1) * channels] = tw_ref[k]
        for f in range(count):
            here = [k for k in range(taps) if f - k >= 0]
            weights = w_s[:, : len(here) * channels]

            def value_of(ref, at):
                delayed = jnp.concatenate(
                    [ref[f - k, 0, :, at : at + span] for k in here], axis=0
                )
                value = jnp.dot(weights, delayed, preferred_element_type=F32)
                return (value + ref[f, 0, :, at : at + span].astype(F32)).astype(BF16)

            for at in range(0, inside, span):
                out_ref[f, 0, :, cols + at : cols + at + span] = value_of(inner_ref, at)
            value = value_of(outer_ref, 0)
            out_ref[f, 0, :, :cols] = value[:, :cols]
            out_ref[f, 0, :, pixels - cols :] = value[:, cols:]

    def part(width):
        return pl.BlockSpec((count, 1, channels, width), lambda i: (0, parity, 0, 0))

    in_specs = [
        part(inside),
        part(span),
        pl.BlockSpec(temporal_weight.shape, lambda i: (0, 0, 0)),
    ]
    operands = [
        inner.reshape(count, 2, channels, inside),
        outer.reshape(count, 2, channels, span),
        temporal_weight,
    ]
    more = {}
    if rest is not None:
        in_specs.append(pl.BlockSpec(memory_space=pl.ANY))
        operands.append(rest)
        more["input_output_aliases"] = {3: 0}
    return call(
        kernel,
        "temporal_output",
        jax.ShapeDtypeStruct((count, 2, channels, pixels), BF16),
        8 * taps * channels * inner.size,
        scratch=[pltpu.VMEM((channels, taps * channels), BF16)],
        grid=(1,),
        in_specs=in_specs,
        out_specs=part(pixels),
        **more,
    )(*operands)


def gelu_and_slope(values):
    scale = 0.7978845608
    cubic = (scale * 0.044715) * (values * values)
    bent = jnp.tanh(values * (scale + cubic))
    half = 0.5 + 0.5 * bent
    active = values * half
    slope = half * (1.0 + (values - active) * (2.0 * scale + 6.0 * cubic))
    return active, slope


def layer(name, listed, lines, halo, cotangent, back_grad, weights, bias_tile, taps, sums):
    owners, members, local, rows, width, cols = lines.shape
    total = owners * local
    channels = members * width
    pixels = len(listed) * cols
    final = sums is not None
    packed = (9 + taps + 1) // 2 * channels + 16
    half = packed // 2
    trio = 3 * channels
    joined = local if pixels <= 512 else 1
    near_frames = 4
    ahead = near_frames + taps - 1
    pieces_of = []
    for at, r in enumerate(listed):
        if pieces_of and pieces_of[-1][0] + pieces_of[-1][2] == r:
            pieces_of[-1][2] += 1
        else:
            pieces_of.append([r, at, 1])

    def kernel(*refs):
        refs = list(refs)
        if halo is not None:
            side_ref, near_ref, far_ref = refs[:3]
            refs = refs[3:]
        x_ref, cot_ref, back_ref, w_ref, bias_ref = refs[:5]
        refs = refs[5:]
        if final:
            before = refs[:3]
            refs = refs[3:]
        hid_ref = refs.pop(0)
        results = refs[: 2 if final else 3]
        refs = refs[2 if final else 3 :]
        gp_s, pair_s, cot_s, back_s, cot_sems, back_sems = refs[:6]
        refs = refs[6:]

        def fetch(source, target, frames, sems):
            return [
                pltpu.make_async_copy(
                    source.at[frames, :, :, pl.ds(start * cols, count * cols)],
                    target.at[frames, :, :, pl.ds(at * cols, count * cols)],
                    sems.at[p],
                )
                for p, (start, at, count) in enumerate(pieces_of)
            ]

        back_copies = [
            fetch(back_ref, back_s, pl.ds(f, 1), back_sems.at[f]) for f in range(owners)
        ]
        cot_copies = fetch(cot_ref, cot_s, pl.ds(0, owners), cot_sems)
        for copies in back_copies + [cot_copies]:
            for copy in copies:
                copy.start()

        if halo is not None:
            top_s, bottom_s = refs[:2]
            refs = refs[2:]

            @pl.when(side_ref[0] == 0)
            def _():
                top_s[...] = far_ref[...]
                bottom_s[...] = near_ref[...]

            @pl.when(side_ref[0] == 1)
            def _():
                top_s[...] = near_ref[...]
                bottom_s[...] = far_ref[...]

        lane = lax.broadcasted_iota(jnp.int32, (channels, cols), 1)
        first = lane == 0
        last = lane == cols - 1

        def shifted(tile, by):
            if by == 1:
                return jnp.where(first, 0.0, pltpu.roll(tile, 1, 1))
            return jnp.where(last, 0.0, pltpu.roll(tile, cols - 1, 1))

        def row(f, j, r):
            if r < 0:
                return [top_s[f, c, j] for c in range(members)]
            if r == rows:
                return [bottom_s[f, c, j] for c in range(members)]
            return [x_ref[f, c, j, r] for c in range(members)]

        def three_rows(f, j, r):
            return jnp.concatenate(row(f, j, r - 1) + row(f, j, r) + row(f, j, r + 1), axis=0)

        bias_sum = None
        for f in range(owners):
            for copy in back_copies[f]:
                copy.wait()
            for j0 in range(0, local, joined):
                sources = [(j, n, r) for j in range(j0, j0 + joined) for n, r in enumerate(listed)]
                stack = jnp.concatenate([three_rows(f, j, r) for j, n, r in sources], axis=1)
                conv = jnp.dot(w_ref[...], stack, preferred_element_type=F32)
                for u, (j, n, r) in enumerate(sources):
                    lo = u * cols
                    span = slice(n * cols, n * cols + cols)
                    at = (f * local + j) * pixels + n * cols
                    place = slice(at, at + cols)
                    pre = (
                        shifted(conv[:channels, lo : lo + cols], 1)
                        + conv[channels : 2 * channels, lo : lo + cols]
                        + shifted(conv[2 * channels :, lo : lo + cols], -1)
                        + bias_ref[...]
                    )
                    active, slope = gelu_and_slope(pre)
                    hid_ref[f, j, :, span] = active.astype(BF16)
                    rounded = (back_s[f, j, :, span].astype(F32) * slope).astype(BF16)
                    grad = rounded.astype(F32)
                    bias_sum = grad if bias_sum is None else bias_sum + grad
                    gp_s[0:channels, place] = shifted(grad, -1).astype(BF16)
                    gp_s[channels : 2 * channels, place] = rounded
                    gp_s[2 * channels :, place] = shifted(grad, 1).astype(BF16)
        whole = jnp.concatenate(
            [
                three_rows(f, j, r)
                for f in range(owners)
                for j in range(local)
                for r in listed
            ],
            axis=1,
        )
        spatial = lax.dot_general(gp_s[...], whole, LANES_IN_LANES, preferred_element_type=F32)

        for copy in cot_copies:
            copy.wait()
        cot_s[pl.ds(owners, taps - 1)] = jnp.zeros((taps - 1, local, channels, pixels), BF16)
        fresh = True
        for j in range(local):
            for f in range(0, owners, near_frames):
                pairs = lax.dot_general(
                    cot_s[f : f + ahead, j].reshape(ahead * channels, pixels),
                    hid_ref[f : f + near_frames, j].reshape(near_frames * channels, pixels),
                    LANES_IN_LANES,
                    preferred_element_type=F32,
                )
                if fresh:
                    pair_s[...] = pairs
                else:
                    pair_s[...] += pairs
                fresh = False
        temporal = []
        for k in range(taps):
            block = None
            for a in range(near_frames):
                more = pair_s[
                    (a + k) * channels : (a + k + 1) * channels, a * channels : (a + 1) * channels
                ]
                block = more if block is None else block + more
            temporal.append(block)

        if final:
            gs_s, pack_s = refs
            gs_s[...] = spatial + before[0][...]
            pieces = []
            for q in range(3):
                for s in range(3):
                    pieces.append(
                        gs_s[s * channels : (s + 1) * channels, q * channels : (q + 1) * channels]
                    )
            for k in range(taps):
                pieces.append(temporal[k] + before[1][k])
            for p in range(len(pieces) // 2):
                pack_s[p * channels : (p + 1) * channels] = jnp.concatenate(
                    pieces[2 * p : 2 * p + 2], axis=1
                )
            base = len(pieces) // 2 * channels
            column = jnp.sum(jnp.transpose(bias_sum + before[2][...]), axis=0, keepdims=True)
            pack_s[base:] = jnp.zeros((packed - base, 2 * channels), F32)
            pack_s[base : base + 1, 0:channels] = column
            mine_ref, other_ref = results
            at = side_ref[0]
            mine_ref[...] = pack_s[pl.ds(pl.multiple_of(at * half, 8), half)]
            other_ref[...] = pack_s[pl.ds(pl.multiple_of((1 - at) * half, 8), half)]
        else:
            gs_ref, gt_ref, gb_ref = results
            gs_ref[...] = spatial
            for k in range(taps):
                gt_ref[k] = temporal[k]
            gb_ref[...] = bias_sum

    view = (owners, local) + cotangent.shape[1:]
    operands = [
        lines,
        pltpu.with_memory_space_constraint(cotangent.reshape(view), pltpu.HBM),
        pltpu.with_memory_space_constraint(back_grad.reshape(view), pltpu.HBM),
        weights,
        bias_tile,
    ]
    in_specs = [ON_CHIP, IN_HBM, IN_HBM, ON_CHIP, ON_CHIP]
    shapes = [jax.ShapeDtypeStruct((owners, local, channels, pixels), BF16)]
    square = (trio, trio)
    slab = (taps, channels, channels)
    tile = (channels, cols)
    scratch = [
        pltpu.VMEM((trio, total * pixels), BF16),
        pltpu.VMEM((ahead * channels, near_frames * channels), F32),
        pltpu.VMEM((owners + taps - 1, local, channels, pixels), BF16),
        pltpu.VMEM((owners, local, channels, pixels), BF16),
        pltpu.SemaphoreType.DMA((len(pieces_of),)),
        pltpu.SemaphoreType.DMA((owners, len(pieces_of))),
    ]
    if halo is not None:
        operands = list(halo) + operands
        in_specs = [SCALARS, ON_CHIP, ON_CHIP] + in_specs
        scratch += [pltpu.VMEM((owners, members, local, width, cols), BF16)] * 2
    if final:
        operands += list(sums)
        in_specs += [ON_CHIP] * 3
        shapes += [jax.ShapeDtypeStruct((half, 2 * channels), F32)] * 2
        scratch += [pltpu.VMEM(square, F32), pltpu.VMEM((packed, 2 * channels), F32)]
    else:
        shapes += [jax.ShapeDtypeStruct(s, F32) for s in (square, slab, tile)]
    hidden, *rest = call(
        kernel,
        name,
        tuple(shapes),
        8 * (2 * 9 + taps) * channels * total * channels * pixels,
        scratch=scratch,
        in_specs=in_specs,
        out_specs=tuple(ON_CHIP for _ in shapes),
    )(*operands)
    return [hidden.reshape(total, channels, pixels)] + rest


def sum_over_devices(mine, other, owners, beside, beneath):
    part = mine + lax.ppermute(other, BOTH, beside)
    bit = 1
    while bit < owners:
        part = part + lax.ppermute(part, "frame", [(i, i ^ bit) for i in range(owners)])
        if bit > 1 and beneath:
            part = beneath.pop(0)(part)
        bit *= 2
    return part


def unpack(side, mine, other, taps, channels):
    half = mine.shape[0]

    def kernel(side_ref, mine_ref, other_ref, gs_ref, gb_ref, gt_ref, pack_s):
        at = side_ref[0]
        pack_s[pl.ds(pl.multiple_of(at * half, 8), half)] = mine_ref[...]
        pack_s[pl.ds(pl.multiple_of((1 - at) * half, 8), half)] = other_ref[...]
        for n in range(9 + taps):
            p, u = n // 2, n % 2
            piece = pack_s[p * channels : (p + 1) * channels, u * channels : (u + 1) * channels]
            if n < 9:
                gs_ref[n] = piece
            else:
                gt_ref[n - 9] = piece
        base = (9 + taps) // 2 * channels
        gb_ref[...] = pack_s[base : base + 1, 0:channels]

    return call(
        kernel,
        "unpack",
        (
            jax.ShapeDtypeStruct((9, channels, channels), F32),
            jax.ShapeDtypeStruct((1, channels), F32),
            jax.ShapeDtypeStruct((taps, channels, channels), F32),
        ),
        mine.size,
        scratch=[pltpu.VMEM((2 * half, 2 * channels), F32)],
        in_specs=[SCALARS, ON_CHIP, ON_CHIP],
    )(side, mine, other)


def make_body(owners, members):
    count = owners * members
    beside = [(i, i ^ 1) for i in range(count)]
    beyond = [(i, i - 1) for i in range(2, count, 2)] + [(i, i + 1) for i in range(1, count - 1, 2)]

    def body(frames, spatial_weight, spatial_bias, temporal_weight, cotangent):
        channels = spatial_weight.shape[1]
        taps = temporal_weight.shape[0]
        cols = frames.shape[3]
        side = lax.axis_index("chan").astype(jnp.int32).reshape(1)
        lines = lax.all_to_all(pack(frames, count), BOTH, split_axis=0, concat_axis=0, tiled=True)
        lines = lines.reshape((owners, members) + lines.shape[1:])
        rows = lines.shape[3]
        back_grad, weights, bias_tile = prepare(
            cotangent, temporal_weight, spatial_weight, spatial_bias.reshape(1, channels), cols
        )
        near_row, far_row = edge_rows(side, lines)
        near = lax.ppermute(near_row, BOTH, beside)
        far = lax.ppermute(far_row, BOTH, beyond)
        shared = (cotangent, back_grad, weights, bias_tile, taps)
        inside = list(range(1, rows - 1))
        inner, *sums = layer("layer_inside", inside, lines, None, *shared, None)
        halo = (side, near, far)
        outer, mine, other = layer("layer_edges", [0, rows - 1], lines, halo, *shared, sums)
        made = []

        def output_of(parity):
            def step(part):
                value = temporal_output(inner, outer, temporal_weight, parity, *made)
                part, value = lax.optimization_barrier((part, value))
                made[:] = [value]
                return part

            return step

        part = sum_over_devices(mine, other, owners, beside, [output_of(0), output_of(1)])
        rest = lax.ppermute(part, BOTH, beside)
        grad_spatial, grad_bias, grad_temporal = unpack(side, part, rest, taps, channels)
        return (
            made[0].reshape(cotangent.shape),
            grad_spatial,
            grad_bias.reshape(channels),
            grad_temporal,
        )

    return body


def solution(mesh):
    return jax.shard_map(
        make_body(mesh.shape["frame"], mesh.shape["chan"]),
        mesh=mesh,
        in_specs=(
            P(("groups", "frame"), "chan", None, None),
            P(),
            P(),
            P(),
            P("groups", None, ("frame", "chan")),
        ),
        out_specs=(
            P("groups", None, ("frame", "chan")),
            P("groups", None, None),
            P("groups"),
            P("groups", None, None),
        ),
        check_vma=False,
    )
```

```python
import math

import jax
import jax.numpy as jnp
from jax import lax
from jax.experimental import pallas as pl
from jax.experimental.pallas import tpu as pltpu
from jax.sharding import PartitionSpec as P

FRAME_DILATION = 2
INSIDE_FRAMES = 8
EDGE_FRAMES = 8
PACK_ROWS = 16
BOTH = ("frame", "chan")
F32 = jnp.float32
BF16 = jnp.bfloat16
LANES_IN_LANES = (((1,), (1,)), ((), ()))


def call(
    kernel, name, out_shape, flops, scratch=(), grid=None, in_specs=None, out_specs=None, **more
):
    shapes = out_shape if isinstance(out_shape, tuple) else (out_shape,)
    nbytes = sum(2 * math.prod(s.shape) * jnp.dtype(s.dtype).itemsize for s in shapes)
    cost = pl.CostEstimate(flops=flops, transcendentals=0, bytes_accessed=nbytes)
    params = dict(out_shape=out_shape, scratch_shapes=list(scratch), name=name, **more)
    params.update(cost_estimate=cost)
    if grid is not None:
        params.update(grid=grid)
    if in_specs is not None:
        params.update(in_specs=in_specs)
    if out_specs is not None:
        params.update(out_specs=out_specs)
    return pl.pallas_call(
        kernel, compiler_params=pltpu.CompilerParams(vmem_limit_bytes=24 << 20), **params
    )


IN_HBM = pl.BlockSpec(memory_space=pltpu.HBM)
ON_CHIP = pl.BlockSpec(memory_space=pltpu.VMEM)
SCALARS = pl.BlockSpec(memory_space=pltpu.SMEM)


def pack(frames, blocks):
    local, width, height, cols = frames.shape
    rows = height // blocks
    tile = PACK_ROWS
    per = tile // rows
    shape = (blocks, local, rows, width, cols)

    def kernel(images_ref, out_ref, images_s, lines_s, in_sems, out_sems):
        def fetch(i):
            part = pl.ds(i * tile, tile)
            return pltpu.make_async_copy(
                images_ref.at[:, :, part], images_s.at[:, :, part], in_sems.at[i]
            )

        def ship(i):
            part = pl.ds(i * per, per)
            return pltpu.make_async_copy(lines_s.at[part], out_ref.at[part], out_sems.at[i])

        steps = range(height // tile)
        for i in steps:
            fetch(i).start()
        for i in steps:
            fetch(i).wait()
            for j in range(local):
                lines = jnp.swapaxes(images_s[j, :, i * tile : (i + 1) * tile], 0, 1)
                for d in range(per):
                    lines_s[i * per + d, j] = lines[d * rows : (d + 1) * rows]
            ship(i).start()
        for i in steps:
            ship(i).wait()

    return call(
        kernel,
        "pack",
        pltpu.HBM(shape, frames.dtype),
        frames.size,
        scratch=[
            pltpu.VMEM(frames.shape, frames.dtype),
            pltpu.VMEM(shape, frames.dtype),
            pltpu.SemaphoreType.DMA((height // tile,)),
            pltpu.SemaphoreType.DMA((height // tile,)),
        ],
        in_specs=[IN_HBM],
        out_specs=IN_HBM,
    )(pltpu.with_memory_space_constraint(frames, pltpu.HBM))


def edge_rows(side, lines):
    owners, members, local, rows, width, cols = lines.shape
    shape = jax.ShapeDtypeStruct((owners, members, local, width, cols), lines.dtype)

    def kernel(side_ref, lines_ref, near_ref, far_ref):
        @pl.when(side_ref[0] == 0)
        def _():
            near_ref[...] = lines_ref[:, :, :, rows - 1]
            far_ref[...] = lines_ref[:, :, :, 0]

        @pl.when(side_ref[0] == 1)
        def _():
            near_ref[...] = lines_ref[:, :, :, 0]
            far_ref[...] = lines_ref[:, :, :, rows - 1]

    return call(
        kernel,
        "edge_rows",
        (shape, shape),
        lines.size,
        in_specs=[SCALARS, ON_CHIP],
        out_specs=(ON_CHIP, ON_CHIP),
    )(side, lines)


def prepare(cotangent, temporal_weight, spatial_weight, bias, cols):
    total, channels, pixels = cotangent.shape
    taps = temporal_weight.shape[0]
    lag = FRAME_DILATION
    span = min(pixels, 256)

    def kernel(cot_ref, tw_ref, sw_ref, bias_ref, out_ref, w_ref, tile_ref, ahead_s):
        @pl.when(pl.program_id(0) == 0)
        def _():
            for k in range(taps):
                turned = jnp.transpose(tw_ref[k].astype(F32))
                ahead_s[:, k * channels : (k + 1) * channels] = turned.astype(BF16)
            for q in range(3):
                for s in range(3):
                    w_ref[s * channels : (s + 1) * channels, q * channels : (q + 1) * channels] = (
                        sw_ref[3 * q + s]
                    )
            tile_ref[...] = jnp.transpose(jnp.broadcast_to(bias_ref[...], (cols, channels)))

        for t in range(total):
            here = [k for k in range(taps) if t + k * lag < total]
            weights = ahead_s[:, : len(here) * channels]
            ahead = jnp.concatenate([cot_ref[t + k * lag] for k in here], axis=0)
            grad = jnp.dot(weights, ahead, preferred_element_type=F32)
            out_ref[t] = (grad + cot_ref[t].astype(F32)).astype(BF16)

    def fixed(shape):
        return pl.BlockSpec(shape, lambda n: (0,) * len(shape))

    trio = (3 * channels, 3 * channels)
    part = pl.BlockSpec((total, channels, span), lambda n: (0, 0, n))
    return call(
        kernel,
        "prepare",
        (
            pltpu.HBM(cotangent.shape, BF16),
            jax.ShapeDtypeStruct(trio, BF16),
            jax.ShapeDtypeStruct((channels, cols), F32),
        ),
        8 * taps * channels * cotangent.size,
        scratch=[pltpu.VMEM((channels, taps * channels), BF16)],
        grid=(pixels // span,),
        in_specs=[
            part,
            fixed(temporal_weight.shape),
            fixed(spatial_weight.shape),
            fixed(bias.shape),
        ],
        out_specs=(
            part,
            fixed(trio),
            fixed((channels, cols)),
        ),
    )(
        pltpu.with_memory_space_constraint(cotangent, pltpu.HBM),
        temporal_weight,
        spatial_weight,
        bias,
    )


def temporal_output(inner, outer, temporal_weight, parity, rest=None):
    total, channels, inside = inner.shape
    span = outer.shape[2]
    cols = span // 2
    count = total // 2
    pixels = inside + span
    taps = temporal_weight.shape[0]

    def kernel(*refs):
        inner_ref, outer_ref, tw_ref, out_ref, w_s = refs[0], refs[1], refs[2], refs[-2], refs[-1]
        for k in range(taps):
            w_s[:, k * channels : (k + 1) * channels] = tw_ref[k]
        for f in range(count):
            here = [k for k in range(taps) if f - k >= 0]
            weights = w_s[:, : len(here) * channels]

            def value_of(ref, at):
                delayed = jnp.concatenate(
                    [ref[f - k, 0, :, at : at + span] for k in here], axis=0
                )
                value = jnp.dot(weights, delayed, preferred_element_type=F32)
                return (value + ref[f, 0, :, at : at + span].astype(F32)).astype(BF16)

            for at in range(0, inside, span):
                out_ref[f, 0, :, cols + at : cols + at + span] = value_of(inner_ref, at)
            value = value_of(outer_ref, 0)
            out_ref[f, 0, :, :cols] = value[:, :cols]
            out_ref[f, 0, :, pixels - cols :] = value[:, cols:]

    def part(width):
        return pl.BlockSpec((count, 1, channels, width), lambda i: (0, parity, 0, 0))

    in_specs = [
        part(inside),
        part(span),
        pl.BlockSpec(temporal_weight.shape, lambda i: (0, 0, 0)),
    ]
    operands = [
        inner.reshape(count, 2, channels, inside),
        outer.reshape(count, 2, channels, span),
        temporal_weight,
    ]
    more = {}
    if rest is not None:
        in_specs.append(pl.BlockSpec(memory_space=pl.ANY))
        operands.append(rest)
        more["input_output_aliases"] = {3: 0}
    return call(
        kernel,
        "temporal_output",
        jax.ShapeDtypeStruct((count, 2, channels, pixels), BF16),
        8 * taps * channels * inner.size,
        scratch=[pltpu.VMEM((channels, taps * channels), BF16)],
        grid=(1,),
        in_specs=in_specs,
        out_specs=part(pixels),
        **more,
    )(*operands)


def gelu_and_slope(values):
    scale = 0.7978845608
    cubic = (scale * 0.044715) * (values * values)
    bent = jnp.tanh(values * (scale + cubic))
    half = 0.5 + 0.5 * bent
    active = values * half
    slope = half * (1.0 + (values - active) * (2.0 * scale + 6.0 * cubic))
    return active, slope


def layer(name, listed, lines, halo, cotangent, back_grad, weights, bias_tile, taps, sums, per):
    owners, members, local, rows, width, cols = lines.shape
    total = owners * local
    channels = members * width
    pixels = len(listed) * cols
    final = sums is not None
    packed = (9 + taps + 1) // 2 * channels + 16
    half = packed // 2
    trio = 3 * channels
    joined = local if pixels <= 512 else 1
    near_frames = 4
    ahead = near_frames + taps - 1
    pieces_of = []
    for at, r in enumerate(listed):
        if pieces_of and pieces_of[-1][0] + pieces_of[-1][2] == r:
            pieces_of[-1][2] += 1
        else:
            pieces_of.append([r, at, 1])
    def kernel(*refs):
        refs = list(refs)
        if halo is not None:
            side_ref, near_ref, far_ref = refs[:3]
            refs = refs[3:]
        x_ref, cot_ref, back_ref, w_ref, bias_ref = refs[:5]
        refs = refs[5:]
        if final:
            before = refs[:3]
            refs = refs[3:]
        hid_ref = refs.pop(0)
        results = refs[: 2 if final else 3]
        refs = refs[2 if final else 3 :]
        gp_s, pair_s, gs_s, gb_s, cot_s, cot_sems = refs[:6]
        refs = refs[6:]
        cot_copies = [
            pltpu.make_async_copy(
                cot_ref.at[:, :, :, pl.ds(start * cols, count * cols)],
                cot_s.at[:, :, :, pl.ds(at * cols, count * cols)],
                cot_sems.at[p],
            )
            for p, (start, at, count) in enumerate(pieces_of)
        ]
        for copy in cot_copies:
            copy.start()

        if halo is not None:
            top_s, bottom_s = refs[:2]
            refs = refs[2:]

            @pl.when(side_ref[0] == 0)
            def _():
                top_s[...] = far_ref[...]
                bottom_s[...] = near_ref[...]

            @pl.when(side_ref[0] == 1)
            def _():
                top_s[...] = near_ref[...]
                bottom_s[...] = far_ref[...]

        lane = lax.broadcasted_iota(jnp.int32, (channels, cols), 1)
        first = lane == 0
        last = lane == cols - 1

        def shifted(tile, by):
            if by == 1:
                return jnp.where(first, 0.0, pltpu.roll(tile, 1, 1))
            return jnp.where(last, 0.0, pltpu.roll(tile, cols - 1, 1))

        def row(f, j, r):
            if r < 0:
                return [top_s[f, c, j] for c in range(members)]
            if r == rows:
                return [bottom_s[f, c, j] for c in range(members)]
            return [x_ref[f, c, j, r] for c in range(members)]

        def three_rows(f, j, r):
            return jnp.concatenate(row(f, j, r - 1) + row(f, j, r) + row(f, j, r + 1), axis=0)

        if final:
            gs_s[...] = before[0][...]
            gb_s[...] = before[2][...]
        else:
            gs_s[...] = jnp.zeros_like(gs_s)
            gb_s[...] = jnp.zeros_like(gb_s)

        def some_frames(i, carry):
            bias_sum = None
            for p in range(per):
                f = i * per + p
                for j0 in range(0, local, joined):
                    sources = [
                        (j, n, r) for j in range(j0, j0 + joined) for n, r in enumerate(listed)
                    ]
                    stack = jnp.concatenate([three_rows(f, j, r) for j, n, r in sources], axis=1)
                    conv = jnp.dot(w_ref[...], stack, preferred_element_type=F32)
                    for u, (j, n, r) in enumerate(sources):
                        lo = u * cols
                        span = slice(n * cols, n * cols + cols)
                        at = (p * local + j) * pixels + n * cols
                        place = slice(at, at + cols)
                        pre = (
                            shifted(conv[:channels, lo : lo + cols], 1)
                            + conv[channels : 2 * channels, lo : lo + cols]
                            + shifted(conv[2 * channels :, lo : lo + cols], -1)
                            + bias_ref[...]
                        )
                        active, slope = gelu_and_slope(pre)
                        hid_ref[f, j, :, span] = active.astype(BF16)
                        back = back_ref[f, j, :, r * cols : (r + 1) * cols].astype(F32)
                        rounded = (back * slope).astype(BF16)
                        grad = rounded.astype(F32)
                        bias_sum = grad if bias_sum is None else bias_sum + grad
                        gp_s[0:channels, place] = shifted(grad, -1).astype(BF16)
                        gp_s[channels : 2 * channels, place] = rounded
                        gp_s[2 * channels :, place] = shifted(grad, 1).astype(BF16)
            gb_s[...] += bias_sum
            whole = jnp.concatenate(
                [
                    three_rows(i * per + p, j, r)
                    for p in range(per)
                    for j in range(local)
                    for r in listed
                ],
                axis=1,
            )
            gs_s[...] += lax.dot_general(
                gp_s[...], whole, LANES_IN_LANES, preferred_element_type=F32
            )
            return carry

        lax.fori_loop(0, owners // per, some_frames, 0)

        for copy in cot_copies:
            copy.wait()
        pair_s[...] = jnp.zeros_like(pair_s)
        for j in range(local):
            for f in range(0, owners, near_frames):
                count = min(ahead, owners - f)
                pairs = lax.dot_general(
                    cot_s[f : f + count, j].reshape(count * channels, pixels),
                    hid_ref[f : f + near_frames, j].reshape(near_frames * channels, pixels),
                    LANES_IN_LANES,
                    preferred_element_type=F32,
                )
                pair_s[0 : count * channels] += pairs
        temporal = []
        for k in range(taps):
            block = None
            for a in range(near_frames):
                more = pair_s[
                    (a + k) * channels : (a + k + 1) * channels, a * channels : (a + 1) * channels
                ]
                block = more if block is None else block + more
            temporal.append(block)

        if final:
            (pack_s,) = refs
            pieces = []
            for q in range(3):
                for s in range(3):
                    pieces.append(
                        gs_s[s * channels : (s + 1) * channels, q * channels : (q + 1) * channels]
                    )
            for k in range(taps):
                pieces.append(temporal[k] + before[1][k])
            for p in range(len(pieces) // 2):
                pack_s[p * channels : (p + 1) * channels] = jnp.concatenate(
                    pieces[2 * p : 2 * p + 2], axis=1
                )
            base = len(pieces) // 2 * channels
            column = jnp.sum(jnp.transpose(gb_s[...]), axis=0, keepdims=True)
            pack_s[base:] = jnp.zeros((packed - base, 2 * channels), F32)
            pack_s[base : base + 1, 0:channels] = column
            mine_ref, other_ref = results
            at = side_ref[0]
            mine_ref[...] = pack_s[pl.ds(pl.multiple_of(at * half, 8), half)]
            other_ref[...] = pack_s[pl.ds(pl.multiple_of((1 - at) * half, 8), half)]
        else:
            gs_ref, gt_ref, gb_ref = results
            gs_ref[...] = gs_s[...]
            for k in range(taps):
                gt_ref[k] = temporal[k]
            gb_ref[...] = gb_s[...]

    view = (owners, local) + cotangent.shape[1:]
    operands = [
        lines,
        pltpu.with_memory_space_constraint(cotangent.reshape(view), pltpu.HBM),
        back_grad.reshape(view),
        weights,
        bias_tile,
    ]
    in_specs = [ON_CHIP, IN_HBM, ON_CHIP, ON_CHIP, ON_CHIP]
    shapes = [jax.ShapeDtypeStruct((owners, local, channels, pixels), BF16)]
    square = (trio, trio)
    slab = (taps, channels, channels)
    tile = (channels, cols)
    scratch = [
        pltpu.VMEM((trio, per * local * pixels), BF16),
        pltpu.VMEM((ahead * channels, near_frames * channels), F32),
        pltpu.VMEM(square, F32),
        pltpu.VMEM(tile, F32),
        pltpu.VMEM((owners, local, channels, pixels), BF16),
        pltpu.SemaphoreType.DMA((len(pieces_of),)),
    ]
    if halo is not None:
        operands = list(halo) + operands
        in_specs = [SCALARS, ON_CHIP, ON_CHIP] + in_specs
        scratch += [pltpu.VMEM((owners, members, local, width, cols), BF16)] * 2
    if final:
        operands += list(sums)
        in_specs += [ON_CHIP] * 3
        shapes += [jax.ShapeDtypeStruct((half, 2 * channels), F32)] * 2
        scratch += [pltpu.VMEM((packed, 2 * channels), F32)]
    else:
        shapes += [jax.ShapeDtypeStruct(s, F32) for s in (square, slab, tile)]
    hidden, *rest = call(
        kernel,
        name,
        tuple(shapes),
        8 * (2 * 9 + taps) * channels * total * channels * pixels,
        scratch=scratch,
        in_specs=in_specs,
        out_specs=tuple(ON_CHIP for _ in shapes),
    )(*operands)
    return [hidden.reshape(total, channels, pixels)] + rest


def sum_over_devices(mine, other, owners, beside, beneath):
    part = mine + lax.ppermute(other, BOTH, beside)
    bit = 1
    while bit < owners:
        part = part + lax.ppermute(part, "frame", [(i, i ^ bit) for i in range(owners)])
        if bit > 1 and beneath:
            part = beneath.pop(0)(part)
        bit *= 2
    return part


def unpack(side, mine, other, taps, channels):
    half = mine.shape[0]

    def kernel(side_ref, mine_ref, other_ref, gs_ref, gb_ref, gt_ref, pack_s):
        at = side_ref[0]
        pack_s[pl.ds(pl.multiple_of(at * half, 8), half)] = mine_ref[...]
        pack_s[pl.ds(pl.multiple_of((1 - at) * half, 8), half)] = other_ref[...]
        for n in range(9 + taps):
            p, u = n // 2, n % 2
            piece = pack_s[p * channels : (p + 1) * channels, u * channels : (u + 1) * channels]
            if n < 9:
                gs_ref[n] = piece
            else:
                gt_ref[n - 9] = piece
        base = (9 + taps) // 2 * channels
        gb_ref[...] = pack_s[base : base + 1, 0:channels]

    return call(
        kernel,
        "unpack",
        (
            jax.ShapeDtypeStruct((9, channels, channels), F32),
            jax.ShapeDtypeStruct((1, channels), F32),
            jax.ShapeDtypeStruct((taps, channels, channels), F32),
        ),
        mine.size,
        scratch=[pltpu.VMEM((2 * half, 2 * channels), F32)],
        in_specs=[SCALARS, ON_CHIP, ON_CHIP],
    )(side, mine, other)


def make_body(owners, members):
    count = owners * members
    beside = [(i, i ^ 1) for i in range(count)]
    beyond = [(i, i - 1) for i in range(2, count, 2)] + [(i, i + 1) for i in range(1, count - 1, 2)]

    def body(frames, spatial_weight, spatial_bias, temporal_weight, cotangent):
        channels = spatial_weight.shape[1]
        taps = temporal_weight.shape[0]
        cols = frames.shape[3]
        side = lax.axis_index("chan").astype(jnp.int32).reshape(1)
        lines = lax.all_to_all(pack(frames, count), BOTH, split_axis=0, concat_axis=0, tiled=True)
        lines = lines.reshape((owners, members) + lines.shape[1:])
        rows = lines.shape[3]
        back_grad, weights, bias_tile = prepare(
            cotangent, temporal_weight, spatial_weight, spatial_bias.reshape(1, channels), cols
        )
        near_row, far_row = edge_rows(side, lines)
        near = lax.ppermute(near_row, BOTH, beside)
        far = lax.ppermute(far_row, BOTH, beyond)
        shared = (cotangent, back_grad, weights, bias_tile, taps)
        inside = list(range(1, rows - 1))
        inner, *sums = layer("layer_inside", inside, lines, None, *shared, None, INSIDE_FRAMES)
        halo = (side, near, far)
        outer, mine, other = layer("layer_edges", [0, rows - 1], lines, halo, *shared, sums, EDGE_FRAMES)
        made = []

        def output_of(parity):
            def step(part):
                value = temporal_output(inner, outer, temporal_weight, parity, *made)
                part, value = lax.optimization_barrier((part, value))
                made[:] = [value]
                return part

            return step

        part = sum_over_devices(mine, other, owners, beside, [output_of(0), output_of(1)])
        rest = lax.ppermute(part, BOTH, beside)
        grad_spatial, grad_bias, grad_temporal = unpack(side, part, rest, taps, channels)
        return (
            made[0].reshape(cotangent.shape),
            grad_spatial,
            grad_bias.reshape(channels),
            grad_temporal,
        )

    return body


def solution(mesh):
    return jax.shard_map(
        make_body(mesh.shape["frame"], mesh.shape["chan"]),
        mesh=mesh,
        in_specs=(
            P(("groups", "frame"), "chan", None, None),
            P(),
            P(),
            P(),
            P("groups", None, ("frame", "chan")),
        ),
        out_specs=(
            P("groups", None, ("frame", "chan")),
            P("groups", None, None),
            P("groups"),
            P("groups", None, None),
        ),
        check_vma=False,
    )
```

```python
import math

import jax
import jax.numpy as jnp
from jax import lax
from jax.experimental import pallas as pl
from jax.experimental.pallas import tpu as pltpu
from jax.sharding import PartitionSpec as P

FRAME_DILATION = 2
INSIDE_FRAMES = 8
EDGE_FRAMES = 8
PACK_ROWS = 16
BOTH = ("frame", "chan")
F32 = jnp.float32
BF16 = jnp.bfloat16
LANES_IN_LANES = (((1,), (1,)), ((), ()))


def call(
    kernel, name, out_shape, flops, scratch=(), grid=None, in_specs=None, out_specs=None, **more
):
    shapes = out_shape if isinstance(out_shape, tuple) else (out_shape,)
    nbytes = sum(2 * math.prod(s.shape) * jnp.dtype(s.dtype).itemsize for s in shapes)
    cost = pl.CostEstimate(flops=flops, transcendentals=0, bytes_accessed=nbytes)
    params = dict(out_shape=out_shape, scratch_shapes=list(scratch), name=name, **more)
    params.update(cost_estimate=cost)
    if grid is not None:
        params.update(grid=grid)
    if in_specs is not None:
        params.update(in_specs=in_specs)
    if out_specs is not None:
        params.update(out_specs=out_specs)
    return pl.pallas_call(
        kernel, compiler_params=pltpu.CompilerParams(vmem_limit_bytes=24 << 20), **params
    )


IN_HBM = pl.BlockSpec(memory_space=pltpu.HBM)
ON_CHIP = pl.BlockSpec(memory_space=pltpu.VMEM)
SCALARS = pl.BlockSpec(memory_space=pltpu.SMEM)


def pack(frames, blocks):
    local, width, height, cols = frames.shape
    rows = height // blocks
    tile = PACK_ROWS
    per = tile // rows
    shape = (blocks, local, rows, width, cols)

    def kernel(images_ref, out_ref, images_s, lines_s, in_sems, out_sems):
        def fetch(i):
            part = pl.ds(i * tile, tile)
            return pltpu.make_async_copy(
                images_ref.at[:, :, part], images_s.at[:, :, part], in_sems.at[i]
            )

        def ship(i):
            part = pl.ds(i * per, per)
            return pltpu.make_async_copy(lines_s.at[part], out_ref.at[part], out_sems.at[i])

        steps = range(height // tile)
        for i in steps:
            fetch(i).start()
        for i in steps:
            fetch(i).wait()
            for j in range(local):
                lines = jnp.swapaxes(images_s[j, :, i * tile : (i + 1) * tile], 0, 1)
                for d in range(per):
                    lines_s[i * per + d, j] = lines[d * rows : (d + 1) * rows]
            ship(i).start()
        for i in steps:
            ship(i).wait()

    return call(
        kernel,
        "pack",
        pltpu.HBM(shape, frames.dtype),
        frames.size,
        scratch=[
            pltpu.VMEM(frames.shape, frames.dtype),
            pltpu.VMEM(shape, frames.dtype),
            pltpu.SemaphoreType.DMA((height // tile,)),
            pltpu.SemaphoreType.DMA((height // tile,)),
        ],
        in_specs=[IN_HBM],
        out_specs=IN_HBM,
    )(pltpu.with_memory_space_constraint(frames, pltpu.HBM))


def edge_rows(side, lines):
    owners, members, local, rows, width, cols = lines.shape
    shape = jax.ShapeDtypeStruct((owners, members, local, width, cols), lines.dtype)

    def kernel(side_ref, lines_ref, near_ref, far_ref):
        @pl.when(side_ref[0] == 0)
        def _():
            near_ref[...] = lines_ref[:, :, :, rows - 1]
            far_ref[...] = lines_ref[:, :, :, 0]

        @pl.when(side_ref[0] == 1)
        def _():
            near_ref[...] = lines_ref[:, :, :, 0]
            far_ref[...] = lines_ref[:, :, :, rows - 1]

    return call(
        kernel,
        "edge_rows",
        (shape, shape),
        lines.size,
        in_specs=[SCALARS, ON_CHIP],
        out_specs=(ON_CHIP, ON_CHIP),
    )(side, lines)


def prepare(cotangent, temporal_weight, spatial_weight, bias, cols):
    total, channels, pixels = cotangent.shape
    taps = temporal_weight.shape[0]
    lag = FRAME_DILATION
    span = min(pixels, 256)

    def kernel(cot_ref, tw_ref, sw_ref, bias_ref, out_ref, w_ref, tile_ref, ahead_s):
        @pl.when(pl.program_id(0) == 0)
        def _():
            for k in range(taps):
                turned = jnp.transpose(tw_ref[k].astype(F32))
                ahead_s[:, k * channels : (k + 1) * channels] = turned.astype(BF16)
            for q in range(3):
                for s in range(3):
                    w_ref[s * channels : (s + 1) * channels, q * channels : (q + 1) * channels] = (
                        sw_ref[3 * q + s]
                    )
            tile_ref[...] = jnp.transpose(jnp.broadcast_to(bias_ref[...], (cols, channels)))

        for t in range(total):
            here = [k for k in range(taps) if t + k * lag < total]
            weights = ahead_s[:, : len(here) * channels]
            ahead = jnp.concatenate([cot_ref[t + k * lag] for k in here], axis=0)
            grad = jnp.dot(weights, ahead, preferred_element_type=F32)
            out_ref[t] = (grad + cot_ref[t].astype(F32)).astype(BF16)

    def fixed(shape):
        return pl.BlockSpec(shape, lambda n: (0,) * len(shape))

    trio = (3 * channels, 3 * channels)
    part = pl.BlockSpec((total, channels, span), lambda n: (0, 0, n))
    return call(
        kernel,
        "prepare",
        (
            pltpu.HBM(cotangent.shape, BF16),
            jax.ShapeDtypeStruct(trio, BF16),
            jax.ShapeDtypeStruct((channels, cols), F32),
        ),
        8 * taps * channels * cotangent.size,
        scratch=[pltpu.VMEM((channels, taps * channels), BF16)],
        grid=(pixels // span,),
        in_specs=[
            part,
            fixed(temporal_weight.shape),
            fixed(spatial_weight.shape),
            fixed(bias.shape),
        ],
        out_specs=(
            part,
            fixed(trio),
            fixed((channels, cols)),
        ),
    )(
        pltpu.with_memory_space_constraint(cotangent, pltpu.HBM),
        temporal_weight,
        spatial_weight,
        bias,
    )


def temporal_output(inner, outer, temporal_weight, parity, rest=None):
    total, channels, inside = inner.shape
    span = outer.shape[2]
    cols = span // 2
    count = total // 2
    pixels = inside + span
    taps = temporal_weight.shape[0]

    def kernel(*refs):
        inner_ref, outer_ref, tw_ref, out_ref, w_s = refs[0], refs[1], refs[2], refs[-2], refs[-1]
        for k in range(taps):
            w_s[:, k * channels : (k + 1) * channels] = tw_ref[k]
        for f in range(count):
            here = [k for k in range(taps) if f - k >= 0]
            weights = w_s[:, : len(here) * channels]

            def value_of(ref, at):
                delayed = jnp.concatenate(
                    [ref[f - k, 0, :, at : at + span] for k in here], axis=0
                )
                value = jnp.dot(weights, delayed, preferred_element_type=F32)
                return (value + ref[f, 0, :, at : at + span].astype(F32)).astype(BF16)

            for at in range(0, inside, span):
                out_ref[f, 0, :, cols + at : cols + at + span] = value_of(inner_ref, at)
            value = value_of(outer_ref, 0)
            out_ref[f, 0, :, :cols] = value[:, :cols]
            out_ref[f, 0, :, pixels - cols :] = value[:, cols:]

    def part(width):
        return pl.BlockSpec((count, 1, channels, width), lambda i: (0, parity, 0, 0))

    in_specs = [
        part(inside),
        part(span),
        pl.BlockSpec(temporal_weight.shape, lambda i: (0, 0, 0)),
    ]
    operands = [
        inner.reshape(count, 2, channels, inside),
        outer.reshape(count, 2, channels, span),
        temporal_weight,
    ]
    more = {}
    if rest is not None:
        in_specs.append(pl.BlockSpec(memory_space=pl.ANY))
        operands.append(rest)
        more["input_output_aliases"] = {3: 0}
    return call(
        kernel,
        "temporal_output",
        jax.ShapeDtypeStruct((count, 2, channels, pixels), BF16),
        8 * taps * channels * inner.size,
        scratch=[pltpu.VMEM((channels, taps * channels), BF16)],
        grid=(1,),
        in_specs=in_specs,
        out_specs=part(pixels),
        **more,
    )(*operands)


def gelu_and_slope(values):
    scale = 0.7978845608
    cubic = (scale * 0.044715) * (values * values)
    bent = jnp.tanh(values * (scale + cubic))
    half = 0.5 + 0.5 * bent
    active = values * half
    slope = half * (1.0 + (values - active) * (2.0 * scale + 6.0 * cubic))
    return active, slope


def layer(name, listed, lines, halo, cotangent, back_grad, weights, bias_tile, taps, sums, per):
    owners, members, local, rows, width, cols = lines.shape
    total = owners * local
    channels = members * width
    pixels = len(listed) * cols
    final = sums is not None
    packed = (9 + taps + 1) // 2 * channels + 16
    half = packed // 2
    trio = 3 * channels
    joined = local if pixels <= 512 else 1
    near_frames = 4
    ahead = near_frames + taps - 1
    pieces_of = []
    for at, r in enumerate(listed):
        if pieces_of and pieces_of[-1][0] + pieces_of[-1][2] == r:
            pieces_of[-1][2] += 1
        else:
            pieces_of.append([r, at, 1])
    def kernel(*refs):
        refs = list(refs)
        if halo is not None:
            side_ref, near_ref, far_ref = refs[:3]
            refs = refs[3:]
        x_ref, cot_ref, back_ref, w_ref, bias_ref = refs[:5]
        refs = refs[5:]
        if final:
            before = refs[:3]
            refs = refs[3:]
        hid_ref = refs.pop(0)
        results = refs[: 2 if final else 3]
        refs = refs[2 if final else 3 :]
        gp_s, pair_s, gs_s, gb_s, cot_s, cot_sems = refs[:6]
        refs = refs[6:]
        cot_copies = [
            pltpu.make_async_copy(
                cot_ref.at[:, :, :, pl.ds(start * cols, count * cols)],
                cot_s.at[:, :, :, pl.ds(at * cols, count * cols)],
                cot_sems.at[p],
            )
            for p, (start, at, count) in enumerate(pieces_of)
        ]
        for copy in cot_copies:
            copy.start()

        if halo is not None:
            top_s, bottom_s = refs[:2]
            refs = refs[2:]

            @pl.when(side_ref[0] == 0)
            def _():
                top_s[...] = far_ref[...]
                bottom_s[...] = near_ref[...]

            @pl.when(side_ref[0] == 1)
            def _():
                top_s[...] = near_ref[...]
                bottom_s[...] = far_ref[...]

        lane = lax.broadcasted_iota(jnp.int32, (channels, cols), 1)
        first = lane == 0
        last = lane == cols - 1

        def shifted(tile, by):
            if by == 1:
                return jnp.where(first, 0.0, pltpu.roll(tile, 1, 1))
            return jnp.where(last, 0.0, pltpu.roll(tile, cols - 1, 1))

        def row(f, j, r):
            if r < 0:
                return [top_s[f, c, j] for c in range(members)]
            if r == rows:
                return [bottom_s[f, c, j] for c in range(members)]
            return [x_ref[f, c, j, r] for c in range(members)]

        def three_rows(f, j, r):
            return jnp.concatenate(row(f, j, r - 1) + row(f, j, r) + row(f, j, r + 1), axis=0)

        if final:
            gs_s[...] = before[0][...]
            gb_s[...] = before[2][...]
        else:
            gs_s[...] = jnp.zeros_like(gs_s)
            gb_s[...] = jnp.zeros_like(gb_s)

        def some_frames(i, carry):
            bias_sum = None
            for p in range(per):
                f = i * per + p
                for j0 in range(0, local, joined):
                    sources = [
                        (j, n, r) for j in range(j0, j0 + joined) for n, r in enumerate(listed)
                    ]
                    stack = jnp.concatenate([three_rows(f, j, r) for j, n, r in sources], axis=1)
                    conv = jnp.dot(w_ref[...], stack, preferred_element_type=F32)
                    for u, (j, n, r) in enumerate(sources):
                        lo = u * cols
                        span = slice(n * cols, n * cols + cols)
                        at = (p * local + j) * pixels + n * cols
                        place = slice(at, at + cols)
                        pre = (
                            shifted(conv[:channels, lo : lo + cols], 1)
                            + conv[channels : 2 * channels, lo : lo + cols]
                            + shifted(conv[2 * channels :, lo : lo + cols], -1)
                            + bias_ref[...]
                        )
                        active, slope = gelu_and_slope(pre)
                        hid_ref[f, j, :, span] = active.astype(BF16)
                        back = back_ref[f, j, :, r * cols : (r + 1) * cols].astype(F32)
                        rounded = (back * slope).astype(BF16)
                        grad = rounded.astype(F32)
                        bias_sum = grad if bias_sum is None else bias_sum + grad
                        gp_s[0:channels, place] = shifted(grad, -1).astype(BF16)
                        gp_s[channels : 2 * channels, place] = rounded
                        gp_s[2 * channels :, place] = shifted(grad, 1).astype(BF16)
            gb_s[...] += bias_sum
            whole = jnp.concatenate(
                [
                    three_rows(i * per + p, j, r)
                    for p in range(per)
                    for j in range(local)
                    for r in listed
                ],
                axis=1,
            )
            gs_s[...] += lax.dot_general(
                gp_s[...], whole, LANES_IN_LANES, preferred_element_type=F32
            )
            return carry

        lax.fori_loop(0, owners // per, some_frames, 0)

        for copy in cot_copies:
            copy.wait()
        pair_s[...] = jnp.zeros_like(pair_s)
        for j in range(local):
            for f in range(0, owners, near_frames):
                count = min(ahead, owners - f)
                pairs = lax.dot_general(
                    cot_s[f : f + count, j].reshape(count * channels, pixels),
                    hid_ref[f : f + near_frames, j].reshape(near_frames * channels, pixels),
                    LANES_IN_LANES,
                    preferred_element_type=F32,
                )
                pair_s[0 : count * channels] += pairs
        temporal = []
        for k in range(taps):
            block = None
            for a in range(near_frames):
                more = pair_s[
                    (a + k) * channels : (a + k + 1) * channels, a * channels : (a + 1) * channels
                ]
                block = more if block is None else block + more
            temporal.append(block)

        if final:
            (pack_s,) = refs
            pieces = []
            for q in range(3):
                for s in range(3):
                    pieces.append(
                        gs_s[s * channels : (s + 1) * channels, q * channels : (q + 1) * channels]
                    )
            for k in range(taps):
                pieces.append(temporal[k] + before[1][k])
            for p in range(len(pieces) // 2):
                pack_s[p * channels : (p + 1) * channels] = jnp.concatenate(
                    pieces[2 * p : 2 * p + 2], axis=1
                )
            base = len(pieces) // 2 * channels
            column = jnp.sum(jnp.transpose(gb_s[...]), axis=0, keepdims=True)
            pack_s[base:] = jnp.zeros((packed - base, 2 * channels), F32)
            pack_s[base : base + 1, 0:channels] = column
            mine_ref, other_ref = results
            at = side_ref[0]
            mine_ref[...] = pack_s[pl.ds(pl.multiple_of(at * half, 8), half)]
            other_ref[...] = pack_s[pl.ds(pl.multiple_of((1 - at) * half, 8), half)]
        else:
            gs_ref, gt_ref, gb_ref = results
            gs_ref[...] = gs_s[...]
            for k in range(taps):
                gt_ref[k] = temporal[k]
            gb_ref[...] = gb_s[...]

    view = (owners, local) + cotangent.shape[1:]
    operands = [
        lines,
        pltpu.with_memory_space_constraint(cotangent.reshape(view), pltpu.HBM),
        back_grad.reshape(view),
        weights,
        bias_tile,
    ]
    in_specs = [ON_CHIP, IN_HBM, ON_CHIP, ON_CHIP, ON_CHIP]
    shapes = [jax.ShapeDtypeStruct((owners, local, channels, pixels), BF16)]
    square = (trio, trio)
    slab = (taps, channels, channels)
    tile = (channels, cols)
    scratch = [
        pltpu.VMEM((trio, per * local * pixels), BF16),
        pltpu.VMEM((ahead * channels, near_frames * channels), F32),
        pltpu.VMEM(square, F32),
        pltpu.VMEM(tile, F32),
        pltpu.VMEM((owners, local, channels, pixels), BF16),
        pltpu.SemaphoreType.DMA((len(pieces_of),)),
    ]
    if halo is not None:
        operands = list(halo) + operands
        in_specs = [SCALARS, ON_CHIP, ON_CHIP] + in_specs
        scratch += [pltpu.VMEM((owners, members, local, width, cols), BF16)] * 2
    if final:
        operands += list(sums)
        in_specs += [ON_CHIP] * 3
        shapes += [jax.ShapeDtypeStruct((half, 2 * channels), F32)] * 2
        scratch += [pltpu.VMEM((packed, 2 * channels), F32)]
    else:
        shapes += [jax.ShapeDtypeStruct(s, F32) for s in (square, slab, tile)]
    hidden, *rest = call(
        kernel,
        name,
        tuple(shapes),
        8 * (2 * 9 + taps) * channels * total * channels * pixels,
        scratch=scratch,
        in_specs=in_specs,
        out_specs=tuple(ON_CHIP for _ in shapes),
    )(*operands)
    return [hidden.reshape(total, channels, pixels)] + rest


def sum_over_devices(mine, other, owners, beside, beneath):
    part = mine + lax.ppermute(other, BOTH, beside)
    bits = [1 << n for n in range(owners.bit_length() - 1)]
    orders = (bits, bits[-1:] + bits[:-1])
    for stage in range(len(bits)):
        pairs = [
            (2 * f + c, 2 * (f ^ orders[c][stage]) + c) for f in range(owners) for c in range(2)
        ]
        part = part + lax.ppermute(part, BOTH, pairs)
        if stage > 0 and beneath:
            part = beneath.pop(0)(part)
    return part


def unpack(side, mine, other, taps, channels):
    half = mine.shape[0]

    def kernel(side_ref, mine_ref, other_ref, gs_ref, gb_ref, gt_ref, pack_s):
        at = side_ref[0]
        pack_s[pl.ds(pl.multiple_of(at * half, 8), half)] = mine_ref[...]
        pack_s[pl.ds(pl.multiple_of((1 - at) * half, 8), half)] = other_ref[...]
        for n in range(9 + taps):
            p, u = n // 2, n % 2
            piece = pack_s[p * channels : (p + 1) * channels, u * channels : (u + 1) * channels]
            if n < 9:
                gs_ref[n] = piece
            else:
                gt_ref[n - 9] = piece
        base = (9 + taps) // 2 * channels
        gb_ref[...] = pack_s[base : base + 1, 0:channels]

    return call(
        kernel,
        "unpack",
        (
            jax.ShapeDtypeStruct((9, channels, channels), F32),
            jax.ShapeDtypeStruct((1, channels), F32),
            jax.ShapeDtypeStruct((taps, channels, channels), F32),
        ),
        mine.size,
        scratch=[pltpu.VMEM((2 * half, 2 * channels), F32)],
        in_specs=[SCALARS, ON_CHIP, ON_CHIP],
    )(side, mine, other)


def make_body(owners, members):
    count = owners * members
    beside = [(i, i ^ 1) for i in range(count)]
    beyond = [(i, i - 1) for i in range(2, count, 2)] + [(i, i + 1) for i in range(1, count - 1, 2)]

    def body(frames, spatial_weight, spatial_bias, temporal_weight, cotangent):
        channels = spatial_weight.shape[1]
        taps = temporal_weight.shape[0]
        cols = frames.shape[3]
        side = lax.axis_index("chan").astype(jnp.int32).reshape(1)
        lines = lax.all_to_all(pack(frames, count), BOTH, split_axis=0, concat_axis=0, tiled=True)
        lines = lines.reshape((owners, members) + lines.shape[1:])
        rows = lines.shape[3]
        back_grad, weights, bias_tile = prepare(
            cotangent, temporal_weight, spatial_weight, spatial_bias.reshape(1, channels), cols
        )
        near_row, far_row = edge_rows(side, lines)
        near = lax.ppermute(near_row, BOTH, beside)
        far = lax.ppermute(far_row, BOTH, beyond)
        shared = (cotangent, back_grad, weights, bias_tile, taps)
        inside = list(range(1, rows - 1))
        inner, *sums = layer("layer_inside", inside, lines, None, *shared, None, INSIDE_FRAMES)
        halo = (side, near, far)
        outer, mine, other = layer("layer_edges", [0, rows - 1], lines, halo, *shared, sums, EDGE_FRAMES)
        made = []

        def output_of(parity):
            def step(part):
                value = temporal_output(inner, outer, temporal_weight, parity, *made)
                part, value = lax.optimization_barrier((part, value))
                made[:] = [value]
                return part

            return step

        part = sum_over_devices(mine, other, owners, beside, [output_of(0), output_of(1)])
        rest = lax.ppermute(part, BOTH, beside)
        grad_spatial, grad_bias, grad_temporal = unpack(side, part, rest, taps, channels)
        return (
            made[0].reshape(cotangent.shape),
            grad_spatial,
            grad_bias.reshape(channels),
            grad_temporal,
        )

    return body


def solution(mesh):
    return jax.shard_map(
        make_body(mesh.shape["frame"], mesh.shape["chan"]),
        mesh=mesh,
        in_specs=(
            P(("groups", "frame"), "chan", None, None),
            P(),
            P(),
            P(),
            P("groups", None, ("frame", "chan")),
        ),
        out_specs=(
            P("groups", None, ("frame", "chan")),
            P("groups", None, None),
            P("groups"),
            P("groups", None, None),
        ),
        check_vma=False,
    )
```

```python
import math

import jax
import jax.numpy as jnp
from jax import lax
from jax.experimental import pallas as pl
from jax.experimental.pallas import tpu as pltpu
from jax.sharding import PartitionSpec as P

FRAME_DILATION = 2
INSIDE_FRAMES = 8
EDGE_FRAMES = 8
PACK_ROWS = 16
BOTH = ("frame", "chan")
F32 = jnp.float32
BF16 = jnp.bfloat16
LANES_IN_LANES = (((1,), (1,)), ((), ()))


def call(
    kernel, name, out_shape, flops, scratch=(), grid=None, in_specs=None, out_specs=None, **more
):
    shapes = out_shape if isinstance(out_shape, tuple) else (out_shape,)
    nbytes = sum(2 * math.prod(s.shape) * jnp.dtype(s.dtype).itemsize for s in shapes)
    cost = pl.CostEstimate(flops=flops, transcendentals=0, bytes_accessed=nbytes)
    params = dict(out_shape=out_shape, scratch_shapes=list(scratch), name=name, **more)
    params.update(cost_estimate=cost)
    if grid is not None:
        params.update(grid=grid)
    if in_specs is not None:
        params.update(in_specs=in_specs)
    if out_specs is not None:
        params.update(out_specs=out_specs)
    return pl.pallas_call(
        kernel, compiler_params=pltpu.CompilerParams(vmem_limit_bytes=24 << 20), **params
    )


IN_HBM = pl.BlockSpec(memory_space=pltpu.HBM)
ON_CHIP = pl.BlockSpec(memory_space=pltpu.VMEM)
SCALARS = pl.BlockSpec(memory_space=pltpu.SMEM)


def pack(frames, blocks):
    local, width, height, cols = frames.shape
    rows = height // blocks
    tile = PACK_ROWS
    per = tile // rows
    shape = (blocks, local, rows, width, cols)

    def kernel(images_ref, out_ref, images_s, lines_s, in_sems, out_sems):
        def fetch(i):
            part = pl.ds(i * tile, tile)
            return pltpu.make_async_copy(
                images_ref.at[:, :, part], images_s.at[:, :, part], in_sems.at[i]
            )

        def ship(i):
            part = pl.ds(i * per, per)
            return pltpu.make_async_copy(lines_s.at[part], out_ref.at[part], out_sems.at[i])

        steps = range(height // tile)
        for i in steps:
            fetch(i).start()
        for i in steps:
            fetch(i).wait()
            for j in range(local):
                lines = jnp.swapaxes(images_s[j, :, i * tile : (i + 1) * tile], 0, 1)
                for d in range(per):
                    lines_s[i * per + d, j] = lines[d * rows : (d + 1) * rows]
            ship(i).start()
        for i in steps:
            ship(i).wait()

    return call(
        kernel,
        "pack",
        pltpu.HBM(shape, frames.dtype),
        frames.size,
        scratch=[
            pltpu.VMEM(frames.shape, frames.dtype),
            pltpu.VMEM(shape, frames.dtype),
            pltpu.SemaphoreType.DMA((height // tile,)),
            pltpu.SemaphoreType.DMA((height // tile,)),
        ],
        in_specs=[IN_HBM],
        out_specs=IN_HBM,
    )(pltpu.with_memory_space_constraint(frames, pltpu.HBM))


def edge_rows(side, lines):
    owners, members, local, rows, width, cols = lines.shape
    shape = jax.ShapeDtypeStruct((owners, members, local, width, cols), lines.dtype)

    def kernel(side_ref, lines_ref, near_ref, far_ref):
        @pl.when(side_ref[0] == 0)
        def _():
            near_ref[...] = lines_ref[:, :, :, rows - 1]
            far_ref[...] = lines_ref[:, :, :, 0]

        @pl.when(side_ref[0] == 1)
        def _():
            near_ref[...] = lines_ref[:, :, :, 0]
            far_ref[...] = lines_ref[:, :, :, rows - 1]

    return call(
        kernel,
        "edge_rows",
        (shape, shape),
        lines.size,
        in_specs=[SCALARS, ON_CHIP],
        out_specs=(ON_CHIP, ON_CHIP),
    )(side, lines)


def prepare(cotangent, temporal_weight, spatial_weight, bias, cols):
    total, channels, pixels = cotangent.shape
    taps = temporal_weight.shape[0]
    lag = FRAME_DILATION
    span = min(pixels, 256)

    def kernel(cot_ref, tw_ref, sw_ref, bias_ref, out_ref, w_ref, tile_ref, ahead_s):
        @pl.when(pl.program_id(0) == 0)
        def _():
            for k in range(taps):
                turned = jnp.transpose(tw_ref[k].astype(F32))
                ahead_s[:, k * channels : (k + 1) * channels] = turned.astype(BF16)
            for q in range(3):
                for s in range(3):
                    w_ref[s * channels : (s + 1) * channels, q * channels : (q + 1) * channels] = (
                        sw_ref[3 * q + s]
                    )
            tile_ref[...] = jnp.transpose(jnp.broadcast_to(bias_ref[...], (cols, channels)))

        for t in range(total):
            here = [k for k in range(taps) if t + k * lag < total]
            weights = ahead_s[:, : len(here) * channels]
            ahead = jnp.concatenate([cot_ref[t + k * lag] for k in here], axis=0)
            grad = jnp.dot(weights, ahead, preferred_element_type=F32)
            out_ref[t] = (grad + cot_ref[t].astype(F32)).astype(BF16)

    def fixed(shape):
        return pl.BlockSpec(shape, lambda n: (0,) * len(shape))

    trio = (3 * channels, 3 * channels)
    part = pl.BlockSpec((total, channels, span), lambda n: (0, 0, n))
    return call(
        kernel,
        "prepare",
        (
            pltpu.HBM(cotangent.shape, BF16),
            jax.ShapeDtypeStruct(trio, BF16),
            jax.ShapeDtypeStruct((channels, cols), F32),
        ),
        8 * taps * channels * cotangent.size,
        scratch=[pltpu.VMEM((channels, taps * channels), BF16)],
        grid=(pixels // span,),
        in_specs=[
            part,
            fixed(temporal_weight.shape),
            fixed(spatial_weight.shape),
            fixed(bias.shape),
        ],
        out_specs=(
            part,
            fixed(trio),
            fixed((channels, cols)),
        ),
    )(
        pltpu.with_memory_space_constraint(cotangent, pltpu.HBM),
        temporal_weight,
        spatial_weight,
        bias,
    )


def temporal_output(inner, outer, temporal_weight, parity, rest=None):
    total, channels, inside = inner.shape
    span = outer.shape[2]
    cols = span // 2
    count = total // 2
    pixels = inside + span
    taps = temporal_weight.shape[0]

    def kernel(*refs):
        inner_ref, outer_ref, tw_ref, out_ref, w_s = refs[0], refs[1], refs[2], refs[-2], refs[-1]
        for k in range(taps):
            w_s[:, k * channels : (k + 1) * channels] = tw_ref[k]
        for f in range(count):
            here = [k for k in range(taps) if f - k >= 0]
            weights = w_s[:, : len(here) * channels]

            def value_of(ref, at):
                delayed = jnp.concatenate(
                    [ref[f - k, 0, :, at : at + span] for k in here], axis=0
                )
                value = jnp.dot(weights, delayed, preferred_element_type=F32)
                return (value + ref[f, 0, :, at : at + span].astype(F32)).astype(BF16)

            for at in range(0, inside, span):
                out_ref[f, 0, :, cols + at : cols + at + span] = value_of(inner_ref, at)
            value = value_of(outer_ref, 0)
            out_ref[f, 0, :, :cols] = value[:, :cols]
            out_ref[f, 0, :, pixels - cols :] = value[:, cols:]

    def part(width):
        return pl.BlockSpec((count, 1, channels, width), lambda i: (0, parity, 0, 0))

    in_specs = [
        part(inside),
        part(span),
        pl.BlockSpec(temporal_weight.shape, lambda i: (0, 0, 0)),
    ]
    operands = [
        inner.reshape(count, 2, channels, inside),
        outer.reshape(count, 2, channels, span),
        temporal_weight,
    ]
    more = {}
    if rest is not None:
        in_specs.append(pl.BlockSpec(memory_space=pl.ANY))
        operands.append(rest)
        more["input_output_aliases"] = {3: 0}
    return call(
        kernel,
        "temporal_output",
        jax.ShapeDtypeStruct((count, 2, channels, pixels), BF16),
        8 * taps * channels * inner.size,
        scratch=[pltpu.VMEM((channels, taps * channels), BF16)],
        grid=(1,),
        in_specs=in_specs,
        out_specs=part(pixels),
        **more,
    )(*operands)


def gelu_and_slope(values):
    scale = 0.7978845608
    cubic = (scale * 0.044715) * (values * values)
    bent = jnp.tanh(values * (scale + cubic))
    half = 0.5 + 0.5 * bent
    active = values * half
    slope = half * (1.0 + (values - active) * (2.0 * scale + 6.0 * cubic))
    return active, slope


def layer(name, listed, lines, halo, cotangent, back_grad, weights, bias_tile, taps, sums, per):
    owners, members, local, rows, width, cols = lines.shape
    total = owners * local
    channels = members * width
    pixels = len(listed) * cols
    final = sums is not None
    packed = (9 + taps + 1) // 2 * channels + 16
    half = packed // 2
    trio = 3 * channels
    joined = local if pixels <= 512 else 1
    near_frames = 4
    ahead = near_frames + taps - 1
    pieces_of = []
    for at, r in enumerate(listed):
        if pieces_of and pieces_of[-1][0] + pieces_of[-1][2] == r:
            pieces_of[-1][2] += 1
        else:
            pieces_of.append([r, at, 1])
    def kernel(*refs):
        refs = list(refs)
        if halo is not None:
            side_ref, near_ref, far_ref = refs[:3]
            refs = refs[3:]
        x_ref, cot_ref, back_ref, w_ref, bias_ref = refs[:5]
        refs = refs[5:]
        if final:
            before = refs[:3]
            refs = refs[3:]
        hid_ref = refs.pop(0)
        results = refs[: 2 if final else 3]
        refs = refs[2 if final else 3 :]
        gp_s, pair_s, gs_s, gb_s, cot_s, cot_sems = refs[:6]
        refs = refs[6:]
        cot_copies = [
            pltpu.make_async_copy(
                cot_ref.at[:, :, :, pl.ds(start * cols, count * cols)],
                cot_s.at[:, :, :, pl.ds(at * cols, count * cols)],
                cot_sems.at[p],
            )
            for p, (start, at, count) in enumerate(pieces_of)
        ]
        for copy in cot_copies:
            copy.start()

        if halo is not None:
            top_s, bottom_s = refs[:2]
            refs = refs[2:]

            @pl.when(side_ref[0] == 0)
            def _():
                top_s[...] = far_ref[...]
                bottom_s[...] = near_ref[...]

            @pl.when(side_ref[0] == 1)
            def _():
                top_s[...] = near_ref[...]
                bottom_s[...] = far_ref[...]

        lane = lax.broadcasted_iota(jnp.int32, (channels, cols), 1)
        first = lane == 0
        last = lane == cols - 1

        def shifted(tile, by):
            if by == 1:
                return jnp.where(first, 0.0, pltpu.roll(tile, 1, 1))
            return jnp.where(last, 0.0, pltpu.roll(tile, cols - 1, 1))

        def row(f, j, r):
            if r < 0:
                return [top_s[f, c, j] for c in range(members)]
            if r == rows:
                return [bottom_s[f, c, j] for c in range(members)]
            return [x_ref[f, c, j, r] for c in range(members)]

        def three_rows(f, j, r):
            return jnp.concatenate(row(f, j, r - 1) + row(f, j, r) + row(f, j, r + 1), axis=0)

        if final:
            gs_s[...] = before[0][...]
            gb_s[...] = before[2][...]
        else:
            gs_s[...] = jnp.zeros_like(gs_s)
            gb_s[...] = jnp.zeros_like(gb_s)

        def some_frames(i, carry):
            bias_sum = None
            for p in range(per):
                f = i * per + p
                for j0 in range(0, local, joined):
                    sources = [
                        (j, n, r) for j in range(j0, j0 + joined) for n, r in enumerate(listed)
                    ]
                    stack = jnp.concatenate([three_rows(f, j, r) for j, n, r in sources], axis=1)
                    conv = jnp.dot(w_ref[...], stack, preferred_element_type=F32)
                    for u, (j, n, r) in enumerate(sources):
                        lo = u * cols
                        span = slice(n * cols, n * cols + cols)
                        at = (p * local + j) * pixels + n * cols
                        place = slice(at, at + cols)
                        pre = (
                            shifted(conv[:channels, lo : lo + cols], 1)
                            + conv[channels : 2 * channels, lo : lo + cols]
                            + shifted(conv[2 * channels :, lo : lo + cols], -1)
                            + bias_ref[...]
                        )
                        active, slope = gelu_and_slope(pre)
                        hid_ref[f, j, :, span] = active.astype(BF16)
                        back = back_ref[f, j, :, r * cols : (r + 1) * cols].astype(F32)
                        rounded = (back * slope).astype(BF16)
                        grad = rounded.astype(F32)
                        bias_sum = grad if bias_sum is None else bias_sum + grad
                        nothing = jnp.zeros_like(rounded)
                        gp_s[0:channels, place] = jnp.where(
                            last, nothing, pltpu.roll(rounded, cols - 1, 1)
                        )
                        gp_s[channels : 2 * channels, place] = rounded
                        gp_s[2 * channels :, place] = jnp.where(
                            first, nothing, pltpu.roll(rounded, 1, 1)
                        )
            gb_s[...] += bias_sum
            whole = jnp.concatenate(
                [
                    three_rows(i * per + p, j, r)
                    for p in range(per)
                    for j in range(local)
                    for r in listed
                ],
                axis=1,
            )
            gs_s[...] += lax.dot_general(
                gp_s[...], whole, LANES_IN_LANES, preferred_element_type=F32
            )
            return carry

        lax.fori_loop(0, owners // per, some_frames, 0)

        for copy in cot_copies:
            copy.wait()
        pair_s[...] = jnp.zeros_like(pair_s)
        for j in range(local):
            for f in range(0, owners, near_frames):
                count = min(ahead, owners - f)
                pairs = lax.dot_general(
                    cot_s[f : f + count, j].reshape(count * channels, pixels),
                    hid_ref[f : f + near_frames, j].reshape(near_frames * channels, pixels),
                    LANES_IN_LANES,
                    preferred_element_type=F32,
                )
                pair_s[0 : count * channels] += pairs
        temporal = []
        for k in range(taps):
            block = None
            for a in range(near_frames):
                more = pair_s[
                    (a + k) * channels : (a + k + 1) * channels, a * channels : (a + 1) * channels
                ]
                block = more if block is None else block + more
            temporal.append(block)

        if final:
            (pack_s,) = refs
            pieces = []
            for q in range(3):
                for s in range(3):
                    pieces.append(
                        gs_s[s * channels : (s + 1) * channels, q * channels : (q + 1) * channels]
                    )
            for k in range(taps):
                pieces.append(temporal[k] + before[1][k])
            for p in range(len(pieces) // 2):
                pack_s[p * channels : (p + 1) * channels] = jnp.concatenate(
                    pieces[2 * p : 2 * p + 2], axis=1
                )
            base = len(pieces) // 2 * channels
            column = jnp.sum(jnp.transpose(gb_s[...]), axis=0, keepdims=True)
            pack_s[base:] = jnp.zeros((packed - base, 2 * channels), F32)
            pack_s[base : base + 1, 0:channels] = column
            mine_ref, other_ref = results
            at = side_ref[0]
            mine_ref[...] = pack_s[pl.ds(pl.multiple_of(at * half, 8), half)]
            other_ref[...] = pack_s[pl.ds(pl.multiple_of((1 - at) * half, 8), half)]
        else:
            gs_ref, gt_ref, gb_ref = results
            gs_ref[...] = gs_s[...]
            for k in range(taps):
                gt_ref[k] = temporal[k]
            gb_ref[...] = gb_s[...]

    view = (owners, local) + cotangent.shape[1:]
    operands = [
        lines,
        pltpu.with_memory_space_constraint(cotangent.reshape(view), pltpu.HBM),
        back_grad.reshape(view),
        weights,
        bias_tile,
    ]
    in_specs = [ON_CHIP, IN_HBM, ON_CHIP, ON_CHIP, ON_CHIP]
    shapes = [jax.ShapeDtypeStruct((owners, local, channels, pixels), BF16)]
    square = (trio, trio)
    slab = (taps, channels, channels)
    tile = (channels, cols)
    scratch = [
        pltpu.VMEM((trio, per * local * pixels), BF16),
        pltpu.VMEM((ahead * channels, near_frames * channels), F32),
        pltpu.VMEM(square, F32),
        pltpu.VMEM(tile, F32),
        pltpu.VMEM((owners, local, channels, pixels), BF16),
        pltpu.SemaphoreType.DMA((len(pieces_of),)),
    ]
    if halo is not None:
        operands = list(halo) + operands
        in_specs = [SCALARS, ON_CHIP, ON_CHIP] + in_specs
        scratch += [pltpu.VMEM((owners, members, local, width, cols), BF16)] * 2
    if final:
        operands += list(sums)
        in_specs += [ON_CHIP] * 3
        shapes += [jax.ShapeDtypeStruct((half, 2 * channels), F32)] * 2
        scratch += [pltpu.VMEM((packed, 2 * channels), F32)]
    else:
        shapes += [jax.ShapeDtypeStruct(s, F32) for s in (square, slab, tile)]
    hidden, *rest = call(
        kernel,
        name,
        tuple(shapes),
        8 * (2 * 9 + taps) * channels * total * channels * pixels,
        scratch=scratch,
        in_specs=in_specs,
        out_specs=tuple(ON_CHIP for _ in shapes),
    )(*operands)
    return [hidden.reshape(total, channels, pixels)] + rest


def sum_over_devices(mine, other, owners, beside, beneath):
    part = mine + lax.ppermute(other, BOTH, beside)
    bits = [1 << n for n in range(owners.bit_length() - 1)]
    orders = (bits, bits[1:] + bits[:1])
    for stage in range(len(bits)):
        pairs = [
            (2 * f + c, 2 * (f ^ orders[c][stage]) + c) for f in range(owners) for c in range(2)
        ]
        part = part + lax.ppermute(part, BOTH, pairs)
        if stage > 0 and beneath:
            part = beneath.pop(0)(part)
    return part


def unpack(side, mine, other, taps, channels):
    half = mine.shape[0]

    def kernel(side_ref, mine_ref, other_ref, gs_ref, gb_ref, gt_ref, pack_s):
        at = side_ref[0]
        pack_s[pl.ds(pl.multiple_of(at * half, 8), half)] = mine_ref[...]
        pack_s[pl.ds(pl.multiple_of((1 - at) * half, 8), half)] = other_ref[...]
        for n in range(9 + taps):
            p, u = n // 2, n % 2
            piece = pack_s[p * channels : (p + 1) * channels, u * channels : (u + 1) * channels]
            if n < 9:
                gs_ref[n] = piece
            else:
                gt_ref[n - 9] = piece
        base = (9 + taps) // 2 * channels
        gb_ref[...] = pack_s[base : base + 1, 0:channels]

    return call(
        kernel,
        "unpack",
        (
            jax.ShapeDtypeStruct((9, channels, channels), F32),
            jax.ShapeDtypeStruct((1, channels), F32),
            jax.ShapeDtypeStruct((taps, channels, channels), F32),
        ),
        mine.size,
        scratch=[pltpu.VMEM((2 * half, 2 * channels), F32)],
        in_specs=[SCALARS, ON_CHIP, ON_CHIP],
    )(side, mine, other)


def make_body(owners, members):
    count = owners * members
    beside = [(i, i ^ 1) for i in range(count)]
    beyond = [(i, i - 1) for i in range(2, count, 2)] + [(i, i + 1) for i in range(1, count - 1, 2)]

    def body(frames, spatial_weight, spatial_bias, temporal_weight, cotangent):
        channels = spatial_weight.shape[1]
        taps = temporal_weight.shape[0]
        cols = frames.shape[3]
        side = lax.axis_index("chan").astype(jnp.int32).reshape(1)
        lines = lax.all_to_all(pack(frames, count), BOTH, split_axis=0, concat_axis=0, tiled=True)
        lines = lines.reshape((owners, members) + lines.shape[1:])
        rows = lines.shape[3]
        back_grad, weights, bias_tile = prepare(
            cotangent, temporal_weight, spatial_weight, spatial_bias.reshape(1, channels), cols
        )
        near_row, far_row = edge_rows(side, lines)
        near = lax.ppermute(near_row, BOTH, beside)
        far = lax.ppermute(far_row, BOTH, beyond)
        shared = (cotangent, back_grad, weights, bias_tile, taps)
        inside = list(range(1, rows - 1))
        inner, *sums = layer("layer_inside", inside, lines, None, *shared, None, INSIDE_FRAMES)
        halo = (side, near, far)
        outer, mine, other = layer("layer_edges", [0, rows - 1], lines, halo, *shared, sums, EDGE_FRAMES)
        made = []

        def output_of(parity):
            def step(part):
                value = temporal_output(inner, outer, temporal_weight, parity, *made)
                part, value = lax.optimization_barrier((part, value))
                made[:] = [value]
                return part

            return step

        part = sum_over_devices(mine, other, owners, beside, [output_of(0), output_of(1)])
        rest = lax.ppermute(part, BOTH, beside)
        grad_spatial, grad_bias, grad_temporal = unpack(side, part, rest, taps, channels)
        return (
            made[0].reshape(cotangent.shape),
            grad_spatial,
            grad_bias.reshape(channels),
            grad_temporal,
        )

    return body


def solution(mesh):
    return jax.shard_map(
        make_body(mesh.shape["frame"], mesh.shape["chan"]),
        mesh=mesh,
        in_specs=(
            P(("groups", "frame"), "chan", None, None),
            P(),
            P(),
            P(),
            P("groups", None, ("frame", "chan")),
        ),
        out_specs=(
            P("groups", None, ("frame", "chan")),
            P("groups", None, None),
            P("groups"),
            P("groups", None, None),
        ),
        check_vma=False,
    )
```

```python
import math

import jax
import jax.numpy as jnp
from jax import lax
from jax.experimental import pallas as pl
from jax.experimental.pallas import tpu as pltpu
from jax.sharding import PartitionSpec as P

FRAME_DILATION = 2
INSIDE_FRAMES = 8
EDGE_FRAMES = 8
PACK_ROWS = 16
BOTH = ("frame", "chan")
F32 = jnp.float32
BF16 = jnp.bfloat16
LANES_IN_LANES = (((1,), (1,)), ((), ()))


def call(
    kernel, name, out_shape, flops, scratch=(), grid=None, in_specs=None, out_specs=None, **more
):
    shapes = out_shape if isinstance(out_shape, tuple) else (out_shape,)
    nbytes = sum(2 * math.prod(s.shape) * jnp.dtype(s.dtype).itemsize for s in shapes)
    cost = pl.CostEstimate(flops=flops, transcendentals=0, bytes_accessed=nbytes)
    params = dict(out_shape=out_shape, scratch_shapes=list(scratch), name=name, **more)
    params.update(cost_estimate=cost)
    if grid is not None:
        params.update(grid=grid)
    if in_specs is not None:
        params.update(in_specs=in_specs)
    if out_specs is not None:
        params.update(out_specs=out_specs)
    return pl.pallas_call(
        kernel, compiler_params=pltpu.CompilerParams(vmem_limit_bytes=24 << 20), **params
    )


IN_HBM = pl.BlockSpec(memory_space=pltpu.HBM)
ON_CHIP = pl.BlockSpec(memory_space=pltpu.VMEM)
SCALARS = pl.BlockSpec(memory_space=pltpu.SMEM)


def pack(frames, blocks):
    local, width, height, cols = frames.shape
    rows = height // blocks
    tile = PACK_ROWS
    per = tile // rows
    shape = (blocks, local, rows, width, cols)

    def kernel(images_ref, out_ref, images_s, lines_s, in_sems, out_sems):
        def fetch(i):
            part = pl.ds(i * tile, tile)
            return pltpu.make_async_copy(
                images_ref.at[:, :, part], images_s.at[:, :, part], in_sems.at[i]
            )

        def ship(i):
            part = pl.ds(i * per, per)
            return pltpu.make_async_copy(lines_s.at[part], out_ref.at[part], out_sems.at[i])

        steps = range(height // tile)
        for i in steps:
            fetch(i).start()
        for i in steps:
            fetch(i).wait()
            for j in range(local):
                lines = jnp.swapaxes(images_s[j, :, i * tile : (i + 1) * tile], 0, 1)
                for d in range(per):
                    lines_s[i * per + d, j] = lines[d * rows : (d + 1) * rows]
            ship(i).start()
        for i in steps:
            ship(i).wait()

    return call(
        kernel,
        "pack",
        pltpu.HBM(shape, frames.dtype),
        frames.size,
        scratch=[
            pltpu.VMEM(frames.shape, frames.dtype),
            pltpu.VMEM(shape, frames.dtype),
            pltpu.SemaphoreType.DMA((height // tile,)),
            pltpu.SemaphoreType.DMA((height // tile,)),
        ],
        in_specs=[IN_HBM],
        out_specs=IN_HBM,
    )(pltpu.with_memory_space_constraint(frames, pltpu.HBM))


def edge_rows(side, lines):
    owners, members, local, rows, width, cols = lines.shape
    shape = jax.ShapeDtypeStruct((owners, members, local, width, cols), lines.dtype)

    def kernel(side_ref, lines_ref, near_ref, far_ref):
        @pl.when(side_ref[0] == 0)
        def _():
            near_ref[...] = lines_ref[:, :, :, rows - 1]
            far_ref[...] = lines_ref[:, :, :, 0]

        @pl.when(side_ref[0] == 1)
        def _():
            near_ref[...] = lines_ref[:, :, :, 0]
            far_ref[...] = lines_ref[:, :, :, rows - 1]

    return call(
        kernel,
        "edge_rows",
        (shape, shape),
        lines.size,
        in_specs=[SCALARS, ON_CHIP],
        out_specs=(ON_CHIP, ON_CHIP),
    )(side, lines)


def prepare(cotangent, temporal_weight, spatial_weight, bias, cols):
    total, channels, pixels = cotangent.shape
    taps = temporal_weight.shape[0]
    lag = FRAME_DILATION
    span = min(pixels, 256)

    def kernel(cot_ref, tw_ref, sw_ref, bias_ref, out_ref, w_ref, tile_ref, ahead_s):
        @pl.when(pl.program_id(0) == 0)
        def _():
            for k in range(taps):
                turned = jnp.transpose(tw_ref[k].astype(F32))
                ahead_s[:, k * channels : (k + 1) * channels] = turned.astype(BF16)
            for q in range(3):
                for s in range(3):
                    w_ref[s * channels : (s + 1) * channels, q * channels : (q + 1) * channels] = (
                        sw_ref[3 * q + s]
                    )
            tile_ref[...] = jnp.transpose(jnp.broadcast_to(bias_ref[...], (cols, channels)))

        for t in range(total):
            here = [k for k in range(taps) if t + k * lag < total]
            weights = ahead_s[:, : len(here) * channels]
            ahead = jnp.concatenate([cot_ref[t + k * lag] for k in here], axis=0)
            grad = jnp.dot(weights, ahead, preferred_element_type=F32)
            out_ref[t] = (grad + cot_ref[t].astype(F32)).astype(BF16)

    def fixed(shape):
        return pl.BlockSpec(shape, lambda n: (0,) * len(shape))

    trio = (3 * channels, 3 * channels)
    part = pl.BlockSpec((total, channels, span), lambda n: (0, 0, n))
    return call(
        kernel,
        "prepare",
        (
            pltpu.HBM(cotangent.shape, BF16),
            jax.ShapeDtypeStruct(trio, BF16),
            jax.ShapeDtypeStruct((channels, cols), F32),
        ),
        8 * taps * channels * cotangent.size,
        scratch=[pltpu.VMEM((channels, taps * channels), BF16)],
        grid=(pixels // span,),
        in_specs=[
            part,
            fixed(temporal_weight.shape),
            fixed(spatial_weight.shape),
            fixed(bias.shape),
        ],
        out_specs=(
            part,
            fixed(trio),
            fixed((channels, cols)),
        ),
    )(
        pltpu.with_memory_space_constraint(cotangent, pltpu.HBM),
        temporal_weight,
        spatial_weight,
        bias,
    )


def temporal_output(inner, outer, temporal_weight, parity, rest=None):
    total, channels, inside = inner.shape
    span = outer.shape[2]
    cols = span // 2
    count = total // 2
    pixels = inside + span
    taps = temporal_weight.shape[0]

    def kernel(*refs):
        inner_ref, outer_ref, tw_ref, out_ref, w_s = refs[0], refs[1], refs[2], refs[-2], refs[-1]
        for k in range(taps):
            w_s[:, k * channels : (k + 1) * channels] = tw_ref[k]
        for f in range(count):
            here = [k for k in range(taps) if f - k >= 0]
            weights = w_s[:, : len(here) * channels]

            def value_of(ref, at):
                delayed = jnp.concatenate(
                    [ref[f - k, 0, :, at : at + span] for k in here], axis=0
                )
                value = jnp.dot(weights, delayed, preferred_element_type=F32)
                return (value + ref[f, 0, :, at : at + span].astype(F32)).astype(BF16)

            for at in range(0, inside, span):
                out_ref[f, 0, :, cols + at : cols + at + span] = value_of(inner_ref, at)
            value = value_of(outer_ref, 0)
            out_ref[f, 0, :, :cols] = value[:, :cols]
            out_ref[f, 0, :, pixels - cols :] = value[:, cols:]

    def part(width):
        return pl.BlockSpec((count, 1, channels, width), lambda i: (0, parity, 0, 0))

    in_specs = [
        part(inside),
        part(span),
        pl.BlockSpec(temporal_weight.shape, lambda i: (0, 0, 0)),
    ]
    operands = [
        inner.reshape(count, 2, channels, inside),
        outer.reshape(count, 2, channels, span),
        temporal_weight,
    ]
    more = {}
    if rest is not None:
        in_specs.append(pl.BlockSpec(memory_space=pl.ANY))
        operands.append(rest)
        more["input_output_aliases"] = {3: 0}
    return call(
        kernel,
        "temporal_output",
        jax.ShapeDtypeStruct((count, 2, channels, pixels), BF16),
        8 * taps * channels * inner.size,
        scratch=[pltpu.VMEM((channels, taps * channels), BF16)],
        grid=(1,),
        in_specs=in_specs,
        out_specs=part(pixels),
        **more,
    )(*operands)


def gelu_and_slope(values):
    scale = 0.7978845608
    cubic = (scale * 0.044715) * (values * values)
    bent = jnp.tanh(values * (scale + cubic))
    half = 0.5 + 0.5 * bent
    active = values * half
    slope = half * (1.0 + (values - active) * (2.0 * scale + 6.0 * cubic))
    return active, slope


def layer(name, listed, lines, halo, cotangent, back_grad, weights, bias_tile, taps, sums, per):
    owners, members, local, rows, width, cols = lines.shape
    total = owners * local
    channels = members * width
    pixels = len(listed) * cols
    final = sums is not None
    packed = (9 + taps + 1) // 2 * channels + 16
    half = packed // 2
    trio = 3 * channels
    joined = local if pixels <= 512 else 1
    near_frames = 4
    ahead = near_frames + taps - 1
    pieces_of = []
    for at, r in enumerate(listed):
        if pieces_of and pieces_of[-1][0] + pieces_of[-1][2] == r:
            pieces_of[-1][2] += 1
        else:
            pieces_of.append([r, at, 1])
    def kernel(*refs):
        refs = list(refs)
        if halo is not None:
            side_ref, near_ref, far_ref = refs[:3]
            refs = refs[3:]
        x_ref, cot_ref, back_ref, w_ref, bias_ref = refs[:5]
        refs = refs[5:]
        if final:
            before = refs[:3]
            refs = refs[3:]
        hid_ref = refs.pop(0)
        results = refs[: 2 if final else 4]
        refs = refs[2 if final else 4 :]
        gp_s, pair_s, gs_s, gb_s = refs[:4]
        refs = refs[4:]
        if final:
            cot_s = cot_ref
        else:
            cot_s, cot_sem = results.pop(), refs.pop(0)
        if not final:
            cot_copy = pltpu.make_async_copy(cot_ref, cot_s, cot_sem)
            cot_copy.start()

        if halo is not None:
            top_s, bottom_s = refs[:2]
            refs = refs[2:]

            @pl.when(side_ref[0] == 0)
            def _():
                top_s[...] = far_ref[...]
                bottom_s[...] = near_ref[...]

            @pl.when(side_ref[0] == 1)
            def _():
                top_s[...] = near_ref[...]
                bottom_s[...] = far_ref[...]

        lane = lax.broadcasted_iota(jnp.int32, (channels, cols), 1)
        first = lane == 0
        last = lane == cols - 1

        def shifted(tile, by):
            if by == 1:
                return jnp.where(first, 0.0, pltpu.roll(tile, 1, 1))
            return jnp.where(last, 0.0, pltpu.roll(tile, cols - 1, 1))

        def row(f, j, r):
            if r < 0:
                return [top_s[f, c, j] for c in range(members)]
            if r == rows:
                return [bottom_s[f, c, j] for c in range(members)]
            return [x_ref[f, c, j, r] for c in range(members)]

        def three_rows(f, j, r):
            return jnp.concatenate(row(f, j, r - 1) + row(f, j, r) + row(f, j, r + 1), axis=0)

        if final:
            gs_s[...] = before[0][...]
            gb_s[...] = before[2][...]
        else:
            gs_s[...] = jnp.zeros_like(gs_s)
            gb_s[...] = jnp.zeros_like(gb_s)

        def some_frames(i, carry):
            bias_sum = None
            for p in range(per):
                f = i * per + p
                for j0 in range(0, local, joined):
                    sources = [
                        (j, n, r) for j in range(j0, j0 + joined) for n, r in enumerate(listed)
                    ]
                    stack = jnp.concatenate([three_rows(f, j, r) for j, n, r in sources], axis=1)
                    conv = jnp.dot(w_ref[...], stack, preferred_element_type=F32)
                    for u, (j, n, r) in enumerate(sources):
                        lo = u * cols
                        span = slice(n * cols, n * cols + cols)
                        at = (p * local + j) * pixels + n * cols
                        place = slice(at, at + cols)
                        pre = (
                            shifted(conv[:channels, lo : lo + cols], 1)
                            + conv[channels : 2 * channels, lo : lo + cols]
                            + shifted(conv[2 * channels :, lo : lo + cols], -1)
                            + bias_ref[...]
                        )
                        active, slope = gelu_and_slope(pre)
                        hid_ref[f, j, :, span] = active.astype(BF16)
                        back = back_ref[f, j, :, r * cols : (r + 1) * cols].astype(F32)
                        rounded = (back * slope).astype(BF16)
                        grad = rounded.astype(F32)
                        bias_sum = grad if bias_sum is None else bias_sum + grad
                        nothing = jnp.zeros_like(rounded)
                        gp_s[0:channels, place] = jnp.where(
                            last, nothing, pltpu.roll(rounded, cols - 1, 1)
                        )
                        gp_s[channels : 2 * channels, place] = rounded
                        gp_s[2 * channels :, place] = jnp.where(
                            first, nothing, pltpu.roll(rounded, 1, 1)
                        )
            gb_s[...] += bias_sum
            whole = jnp.concatenate(
                [
                    three_rows(i * per + p, j, r)
                    for p in range(per)
                    for j in range(local)
                    for r in listed
                ],
                axis=1,
            )
            gs_s[...] += lax.dot_general(
                gp_s[...], whole, LANES_IN_LANES, preferred_element_type=F32
            )
            return carry

        lax.fori_loop(0, owners // per, some_frames, 0)

        if not final:
            cot_copy.wait()

        def reached(f, count, j):
            parts = [
                cot_s[f : f + count, j, :, start * cols : (start + length) * cols]
                for start, at, length in pieces_of
            ]
            joint = parts[0] if len(parts) == 1 else jnp.concatenate(parts, axis=2)
            return joint.reshape(count * channels, pixels)

        pair_s[...] = jnp.zeros_like(pair_s)
        for j in range(local):
            for f in range(0, owners, near_frames):
                count = min(ahead, owners - f)
                pairs = lax.dot_general(
                    reached(f, count, j),
                    hid_ref[f : f + near_frames, j].reshape(near_frames * channels, pixels),
                    LANES_IN_LANES,
                    preferred_element_type=F32,
                )
                pair_s[0 : count * channels] += pairs
        temporal = []
        for k in range(taps):
            block = None
            for a in range(near_frames):
                more = pair_s[
                    (a + k) * channels : (a + k + 1) * channels, a * channels : (a + 1) * channels
                ]
                block = more if block is None else block + more
            temporal.append(block)

        if final:
            (pack_s,) = refs
            pieces = []
            for q in range(3):
                for s in range(3):
                    pieces.append(
                        gs_s[s * channels : (s + 1) * channels, q * channels : (q + 1) * channels]
                    )
            for k in range(taps):
                pieces.append(temporal[k] + before[1][k])
            for p in range(len(pieces) // 2):
                pack_s[p * channels : (p + 1) * channels] = jnp.concatenate(
                    pieces[2 * p : 2 * p + 2], axis=1
                )
            base = len(pieces) // 2 * channels
            column = jnp.sum(jnp.transpose(gb_s[...]), axis=0, keepdims=True)
            pack_s[base:] = jnp.zeros((packed - base, 2 * channels), F32)
            pack_s[base : base + 1, 0:channels] = column
            mine_ref, other_ref = results
            at = side_ref[0]
            mine_ref[...] = pack_s[pl.ds(pl.multiple_of(at * half, 8), half)]
            other_ref[...] = pack_s[pl.ds(pl.multiple_of((1 - at) * half, 8), half)]
        else:
            gs_ref, gt_ref, gb_ref = results
            gs_ref[...] = gs_s[...]
            for k in range(taps):
                gt_ref[k] = temporal[k]
            gb_ref[...] = gb_s[...]

    view = (owners, local) + cotangent.shape[-2:]
    operands = [
        lines,
        cotangent.reshape(view),
        back_grad.reshape(view),
        weights,
        bias_tile,
    ]
    in_specs = [ON_CHIP] * len(operands)
    if not final:
        operands[1] = pltpu.with_memory_space_constraint(operands[1], pltpu.HBM)
        in_specs[1] = IN_HBM
        scratch_last = [pltpu.SemaphoreType.DMA(())]
    else:
        scratch_last = []
    shapes = [jax.ShapeDtypeStruct((owners, local, channels, pixels), BF16)]
    square = (trio, trio)
    slab = (taps, channels, channels)
    tile = (channels, cols)
    scratch = [
        pltpu.VMEM((trio, per * local * pixels), BF16),
        pltpu.VMEM((ahead * channels, near_frames * channels), F32),
        pltpu.VMEM(square, F32),
        pltpu.VMEM(tile, F32),
    ]
    scratch += scratch_last
    if halo is not None:
        operands = list(halo) + operands
        in_specs = [SCALARS, ON_CHIP, ON_CHIP] + in_specs
        scratch += [pltpu.VMEM((owners, members, local, width, cols), BF16)] * 2
    if final:
        operands += list(sums)
        in_specs += [ON_CHIP] * 3
        shapes += [jax.ShapeDtypeStruct((half, 2 * channels), F32)] * 2
        scratch += [pltpu.VMEM((packed, 2 * channels), F32)]
    else:
        shapes += [jax.ShapeDtypeStruct(s, F32) for s in (square, slab, tile)]
        shapes += [jax.ShapeDtypeStruct(view, BF16)]
    hidden, *rest = call(
        kernel,
        name,
        tuple(shapes),
        8 * (2 * 9 + taps) * channels * total * channels * pixels,
        scratch=scratch,
        in_specs=in_specs,
        out_specs=tuple(ON_CHIP for _ in shapes),
    )(*operands)
    return [hidden.reshape(total, channels, pixels)] + rest


def sum_over_devices(mine, other, owners, beside, beneath):
    part = mine + lax.ppermute(other, BOTH, beside)
    bits = [1 << n for n in range(owners.bit_length() - 1)]
    orders = (bits, bits[1:] + bits[:1])
    for stage in range(len(bits)):
        pairs = [
            (2 * f + c, 2 * (f ^ orders[c][stage]) + c) for f in range(owners) for c in range(2)
        ]
        part = part + lax.ppermute(part, BOTH, pairs)
        if stage > 0 and beneath:
            part = beneath.pop(0)(part)
    return part


def unpack(side, mine, other, taps, channels):
    half = mine.shape[0]

    def kernel(side_ref, mine_ref, other_ref, gs_ref, gb_ref, gt_ref, pack_s):
        at = side_ref[0]
        pack_s[pl.ds(pl.multiple_of(at * half, 8), half)] = mine_ref[...]
        pack_s[pl.ds(pl.multiple_of((1 - at) * half, 8), half)] = other_ref[...]
        for n in range(9 + taps):
            p, u = n // 2, n % 2
            piece = pack_s[p * channels : (p + 1) * channels, u * channels : (u + 1) * channels]
            if n < 9:
                gs_ref[n] = piece
            else:
                gt_ref[n - 9] = piece
        base = (9 + taps) // 2 * channels
        gb_ref[...] = pack_s[base : base + 1, 0:channels]

    return call(
        kernel,
        "unpack",
        (
            jax.ShapeDtypeStruct((9, channels, channels), F32),
            jax.ShapeDtypeStruct((1, channels), F32),
            jax.ShapeDtypeStruct((taps, channels, channels), F32),
        ),
        mine.size,
        scratch=[pltpu.VMEM((2 * half, 2 * channels), F32)],
        in_specs=[SCALARS, ON_CHIP, ON_CHIP],
    )(side, mine, other)


def make_body(owners, members):
    count = owners * members
    beside = [(i, i ^ 1) for i in range(count)]
    beyond = [(i, i - 1) for i in range(2, count, 2)] + [(i, i + 1) for i in range(1, count - 1, 2)]

    def body(frames, spatial_weight, spatial_bias, temporal_weight, cotangent):
        channels = spatial_weight.shape[1]
        taps = temporal_weight.shape[0]
        cols = frames.shape[3]
        side = lax.axis_index("chan").astype(jnp.int32).reshape(1)
        lines = lax.all_to_all(pack(frames, count), BOTH, split_axis=0, concat_axis=0, tiled=True)
        lines = lines.reshape((owners, members) + lines.shape[1:])
        rows = lines.shape[3]
        back_grad, weights, bias_tile = prepare(
            cotangent, temporal_weight, spatial_weight, spatial_bias.reshape(1, channels), cols
        )
        near_row, far_row = edge_rows(side, lines)
        far = lax.ppermute(far_row, BOTH, beyond)
        near = lax.ppermute(near_row, BOTH, beside)
        shared = (back_grad, weights, bias_tile, taps)
        inside = list(range(1, rows - 1))
        inner, *sums, cot = layer(
            "layer_inside", inside, lines, None, cotangent, *shared, None, INSIDE_FRAMES
        )
        halo = (side, near, far)
        outer, mine, other = layer(
            "layer_edges", [0, rows - 1], lines, halo, cot, *shared, sums, EDGE_FRAMES
        )
        made = []

        def output_of(parity):
            def step(part):
                value = temporal_output(inner, outer, temporal_weight, parity, *made)
                part, value = lax.optimization_barrier((part, value))
                made[:] = [value]
                return part

            return step

        part = sum_over_devices(mine, other, owners, beside, [output_of(0), output_of(1)])
        rest = lax.ppermute(part, BOTH, beside)
        grad_spatial, grad_bias, grad_temporal = unpack(side, part, rest, taps, channels)
        return (
            made[0].reshape(cotangent.shape),
            grad_spatial,
            grad_bias.reshape(channels),
            grad_temporal,
        )

    return body


def solution(mesh):
    return jax.shard_map(
        make_body(mesh.shape["frame"], mesh.shape["chan"]),
        mesh=mesh,
        in_specs=(
            P(("groups", "frame"), "chan", None, None),
            P(),
            P(),
            P(),
            P("groups", None, ("frame", "chan")),
        ),
        out_specs=(
            P("groups", None, ("frame", "chan")),
            P("groups", None, None),
            P("groups"),
            P("groups", None, None),
        ),
        check_vma=False,
    )
```

```python
import math

import jax
import jax.numpy as jnp
from jax import lax
from jax.experimental import pallas as pl
from jax.experimental.pallas import tpu as pltpu
from jax.sharding import PartitionSpec as P

FRAME_DILATION = 2
INSIDE_FRAMES = 8
EDGE_FRAMES = 8
PACK_ROWS = 16
BOTH = ("frame", "chan")
F32 = jnp.float32
BF16 = jnp.bfloat16
LANES_IN_LANES = (((1,), (1,)), ((), ()))


def call(
    kernel, name, out_shape, flops, scratch=(), grid=None, in_specs=None, out_specs=None, **more
):
    shapes = out_shape if isinstance(out_shape, tuple) else (out_shape,)
    nbytes = sum(2 * math.prod(s.shape) * jnp.dtype(s.dtype).itemsize for s in shapes)
    cost = pl.CostEstimate(flops=flops, transcendentals=0, bytes_accessed=nbytes)
    params = dict(out_shape=out_shape, scratch_shapes=list(scratch), name=name, **more)
    params.update(cost_estimate=cost)
    if grid is not None:
        params.update(grid=grid)
    if in_specs is not None:
        params.update(in_specs=in_specs)
    if out_specs is not None:
        params.update(out_specs=out_specs)
    return pl.pallas_call(
        kernel, compiler_params=pltpu.CompilerParams(vmem_limit_bytes=24 << 20), **params
    )


IN_HBM = pl.BlockSpec(memory_space=pltpu.HBM)
ON_CHIP = pl.BlockSpec(memory_space=pltpu.VMEM)
SCALARS = pl.BlockSpec(memory_space=pltpu.SMEM)


def pack(frames, blocks):
    local, width, height, cols = frames.shape
    rows = height // blocks
    tile = PACK_ROWS
    per = tile // rows
    shape = (blocks, local, rows, width, cols)

    def kernel(images_ref, out_ref, images_s, lines_s, in_sems, out_sems):
        def fetch(i):
            part = pl.ds(i * tile, tile)
            return pltpu.make_async_copy(
                images_ref.at[:, :, part], images_s.at[:, :, part], in_sems.at[i]
            )

        def ship(i):
            part = pl.ds(i * per, per)
            return pltpu.make_async_copy(lines_s.at[part], out_ref.at[part], out_sems.at[i])

        steps = range(height // tile)
        for i in steps:
            fetch(i).start()
        for i in steps:
            fetch(i).wait()
            for j in range(local):
                lines = jnp.swapaxes(images_s[j, :, i * tile : (i + 1) * tile], 0, 1)
                for d in range(per):
                    lines_s[i * per + d, j] = lines[d * rows : (d + 1) * rows]
            ship(i).start()
        for i in steps:
            ship(i).wait()

    return call(
        kernel,
        "pack",
        pltpu.HBM(shape, frames.dtype),
        frames.size,
        scratch=[
            pltpu.VMEM(frames.shape, frames.dtype),
            pltpu.VMEM(shape, frames.dtype),
            pltpu.SemaphoreType.DMA((height // tile,)),
            pltpu.SemaphoreType.DMA((height // tile,)),
        ],
        in_specs=[IN_HBM],
        out_specs=IN_HBM,
    )(pltpu.with_memory_space_constraint(frames, pltpu.HBM))


def edge_rows(side, lines):
    owners, members, local, rows, width, cols = lines.shape
    shape = jax.ShapeDtypeStruct((owners, members, local, width, cols), lines.dtype)

    def kernel(side_ref, lines_ref, near_ref, far_ref):
        @pl.when(side_ref[0] == 0)
        def _():
            near_ref[...] = lines_ref[:, :, :, rows - 1]
            far_ref[...] = lines_ref[:, :, :, 0]

        @pl.when(side_ref[0] == 1)
        def _():
            near_ref[...] = lines_ref[:, :, :, 0]
            far_ref[...] = lines_ref[:, :, :, rows - 1]

    return call(
        kernel,
        "edge_rows",
        (shape, shape),
        lines.size,
        in_specs=[SCALARS, ON_CHIP],
        out_specs=(ON_CHIP, ON_CHIP),
    )(side, lines)


def prepare(cotangent, temporal_weight, spatial_weight, bias, cols):
    total, channels, pixels = cotangent.shape
    taps = temporal_weight.shape[0]
    lag = FRAME_DILATION
    span = min(pixels, 256)

    def kernel(cot_ref, tw_ref, sw_ref, bias_ref, out_ref, w_ref, tile_ref, ahead_s):
        @pl.when(pl.program_id(0) == 0)
        def _():
            for k in range(taps):
                turned = jnp.transpose(tw_ref[k].astype(F32))
                ahead_s[:, k * channels : (k + 1) * channels] = turned.astype(BF16)
            for q in range(3):
                for s in range(3):
                    w_ref[s * channels : (s + 1) * channels, q * channels : (q + 1) * channels] = (
                        sw_ref[3 * q + s]
                    )
            tile_ref[...] = jnp.transpose(jnp.broadcast_to(bias_ref[...], (cols, channels)))

        for t in range(total):
            here = [k for k in range(taps) if t + k * lag < total]
            weights = ahead_s[:, : len(here) * channels]
            ahead = jnp.concatenate([cot_ref[t + k * lag] for k in here], axis=0)
            grad = jnp.dot(weights, ahead, preferred_element_type=F32)
            out_ref[t] = (grad + cot_ref[t].astype(F32)).astype(BF16)

    def fixed(shape):
        return pl.BlockSpec(shape, lambda n: (0,) * len(shape))

    trio = (3 * channels, 3 * channels)
    part = pl.BlockSpec((total, channels, span), lambda n: (0, 0, n))
    return call(
        kernel,
        "prepare",
        (
            pltpu.HBM(cotangent.shape, BF16),
            jax.ShapeDtypeStruct(trio, BF16),
            jax.ShapeDtypeStruct((channels, cols), F32),
        ),
        8 * taps * channels * cotangent.size,
        scratch=[pltpu.VMEM((channels, taps * channels), BF16)],
        grid=(pixels // span,),
        in_specs=[
            part,
            fixed(temporal_weight.shape),
            fixed(spatial_weight.shape),
            fixed(bias.shape),
        ],
        out_specs=(
            part,
            fixed(trio),
            fixed((channels, cols)),
        ),
    )(
        pltpu.with_memory_space_constraint(cotangent, pltpu.HBM),
        temporal_weight,
        spatial_weight,
        bias,
    )


def temporal_output(inner, outer, temporal_weight, parity, rest=None):
    total, channels, inside = inner.shape
    span = outer.shape[2]
    cols = span // 2
    count = total // 2
    pixels = inside + span
    taps = temporal_weight.shape[0]

    def kernel(*refs):
        inner_ref, outer_ref, tw_ref, out_ref, w_s = refs[0], refs[1], refs[2], refs[-2], refs[-1]
        for k in range(taps):
            w_s[:, k * channels : (k + 1) * channels] = tw_ref[k]
        for f in range(count):
            here = [k for k in range(taps) if f - k >= 0]
            weights = w_s[:, : len(here) * channels]

            def value_of(ref, at):
                delayed = jnp.concatenate(
                    [ref[f - k, 0, :, at : at + span] for k in here], axis=0
                )
                value = jnp.dot(weights, delayed, preferred_element_type=F32)
                return (value + ref[f, 0, :, at : at + span].astype(F32)).astype(BF16)

            for at in range(0, inside, span):
                out_ref[f, 0, :, cols + at : cols + at + span] = value_of(inner_ref, at)
            value = value_of(outer_ref, 0)
            out_ref[f, 0, :, :cols] = value[:, :cols]
            out_ref[f, 0, :, pixels - cols :] = value[:, cols:]

    def part(width):
        return pl.BlockSpec((count, 1, channels, width), lambda i: (0, parity, 0, 0))

    in_specs = [
        part(inside),
        part(span),
        pl.BlockSpec(temporal_weight.shape, lambda i: (0, 0, 0)),
    ]
    operands = [
        inner.reshape(count, 2, channels, inside),
        outer.reshape(count, 2, channels, span),
        temporal_weight,
    ]
    more = {}
    if rest is not None:
        in_specs.append(pl.BlockSpec(memory_space=pl.ANY))
        operands.append(rest)
        more["input_output_aliases"] = {3: 0}
    return call(
        kernel,
        "temporal_output",
        jax.ShapeDtypeStruct((count, 2, channels, pixels), BF16),
        8 * taps * channels * inner.size,
        scratch=[pltpu.VMEM((channels, taps * channels), BF16)],
        grid=(1,),
        in_specs=in_specs,
        out_specs=part(pixels),
        **more,
    )(*operands)


def gelu_and_slope(values):
    scale = 0.7978845608
    cubic = (scale * 0.044715) * (values * values)
    bent = jnp.tanh(values * (scale + cubic))
    half = 0.5 + 0.5 * bent
    active = values * half
    slope = half * (1.0 + (values - active) * (2.0 * scale + 6.0 * cubic))
    return active, slope


def layer(name, listed, lines, halo, cotangent, back_grad, weights, bias_tile, taps, sums, per):
    owners, members, local, rows, width, cols = lines.shape
    total = owners * local
    channels = members * width
    pixels = len(listed) * cols
    final = sums is not None
    packed = (9 + taps + 1) // 2 * channels + 16
    half = packed // 2
    trio = 3 * channels
    joined = local if pixels <= 512 else 1
    near_frames = 4
    ahead = near_frames + taps - 1
    pieces_of = []
    for at, r in enumerate(listed):
        if pieces_of and pieces_of[-1][0] + pieces_of[-1][2] == r:
            pieces_of[-1][2] += 1
        else:
            pieces_of.append([r, at, 1])
    def kernel(*refs):
        refs = list(refs)
        if halo is not None:
            side_ref, near_ref, far_ref = refs[:3]
            refs = refs[3:]
        x_ref, cot_ref, back_ref, w_ref, bias_ref = refs[:5]
        refs = refs[5:]
        if final:
            before = refs[:3]
            refs = refs[3:]
        hid_ref = refs.pop(0)
        results = refs[: 2 if final else 4]
        refs = refs[2 if final else 4 :]
        gp_s, pair_s, gs_s, gb_s = refs[:4]
        refs = refs[4:]
        if final:
            cot_s = cot_ref
        else:
            cot_s, cot_sem = results.pop(), refs.pop(0)
        if not final:
            cot_copy = pltpu.make_async_copy(cot_ref, cot_s, cot_sem)
            cot_copy.start()

        if halo is not None:
            top_s, bottom_s = refs[:2]
            refs = refs[2:]

            @pl.when(side_ref[0] == 0)
            def _():
                top_s[...] = far_ref[...]
                bottom_s[...] = near_ref[...]

            @pl.when(side_ref[0] == 1)
            def _():
                top_s[...] = near_ref[...]
                bottom_s[...] = far_ref[...]

        lane = lax.broadcasted_iota(jnp.int32, (channels, cols), 1)
        first = lane == 0
        last = lane == cols - 1

        def shifted(tile, by):
            if by == 1:
                return jnp.where(first, 0.0, pltpu.roll(tile, 1, 1))
            return jnp.where(last, 0.0, pltpu.roll(tile, cols - 1, 1))

        def row(f, j, r):
            if r < 0:
                return [top_s[f, c, j] for c in range(members)]
            if r == rows:
                return [bottom_s[f, c, j] for c in range(members)]
            return [x_ref[f, c, j, r] for c in range(members)]

        def three_rows(f, j, r):
            return jnp.concatenate(row(f, j, r - 1) + row(f, j, r) + row(f, j, r + 1), axis=0)

        if final:
            gs_s[...] = before[0][...]
            gb_s[...] = before[2][...]
        else:
            gs_s[...] = jnp.zeros_like(gs_s)
            gb_s[...] = jnp.zeros_like(gb_s)

        def some_frames(i, carry):
            bias_sum = None
            for p in range(per):
                f = i * per + p
                for j0 in range(0, local, joined):
                    sources = [
                        (j, n, r) for j in range(j0, j0 + joined) for n, r in enumerate(listed)
                    ]
                    stack = jnp.concatenate([three_rows(f, j, r) for j, n, r in sources], axis=1)
                    conv = jnp.dot(w_ref[...], stack, preferred_element_type=F32)
                    for u, (j, n, r) in enumerate(sources):
                        lo = u * cols
                        span = slice(n * cols, n * cols + cols)
                        at = (p * local + j) * pixels + n * cols
                        place = slice(at, at + cols)
                        pre = (
                            shifted(conv[:channels, lo : lo + cols], 1)
                            + conv[channels : 2 * channels, lo : lo + cols]
                            + shifted(conv[2 * channels :, lo : lo + cols], -1)
                            + bias_ref[...]
                        )
                        active, slope = gelu_and_slope(pre)
                        hid_ref[f, j, :, span] = active.astype(BF16)
                        back = back_ref[f, j, :, r * cols : (r + 1) * cols].astype(F32)
                        rounded = (back * slope).astype(BF16)
                        grad = rounded.astype(F32)
                        bias_sum = grad if bias_sum is None else bias_sum + grad
                        nothing = jnp.zeros_like(rounded)
                        gp_s[0:channels, place] = jnp.where(
                            last, nothing, pltpu.roll(rounded, cols - 1, 1)
                        )
                        gp_s[channels : 2 * channels, place] = rounded
                        gp_s[2 * channels :, place] = jnp.where(
                            first, nothing, pltpu.roll(rounded, 1, 1)
                        )
            gb_s[...] += bias_sum
            whole = jnp.concatenate(
                [
                    three_rows(i * per + p, j, r)
                    for p in range(per)
                    for j in range(local)
                    for r in listed
                ],
                axis=1,
            )
            gs_s[...] += lax.dot_general(
                gp_s[...], whole, LANES_IN_LANES, preferred_element_type=F32
            )
            return carry

        lax.fori_loop(0, owners // per, some_frames, 0)

        if not final:
            cot_copy.wait()

        def reached(f, count, j):
            parts = [
                cot_s[f : f + count, j, :, start * cols : (start + length) * cols]
                for start, at, length in pieces_of
            ]
            joint = parts[0] if len(parts) == 1 else jnp.concatenate(parts, axis=2)
            return joint.reshape(count * channels, pixels)

        pair_s[...] = jnp.zeros_like(pair_s)
        for j in range(local):
            for f in range(0, owners, near_frames):
                count = min(ahead, owners - f)
                pairs = lax.dot_general(
                    reached(f, count, j),
                    hid_ref[f : f + near_frames, j].reshape(near_frames * channels, pixels),
                    LANES_IN_LANES,
                    preferred_element_type=F32,
                )
                pair_s[0 : count * channels] += pairs
        temporal = []
        for k in range(taps):
            block = None
            for a in range(near_frames):
                more = pair_s[
                    (a + k) * channels : (a + k + 1) * channels, a * channels : (a + 1) * channels
                ]
                block = more if block is None else block + more
            temporal.append(block)

        if final:
            (pack_s,) = refs
            pieces = []
            for q in range(3):
                for s in range(3):
                    pieces.append(
                        gs_s[s * channels : (s + 1) * channels, q * channels : (q + 1) * channels]
                    )
            for k in range(taps):
                pieces.append(temporal[k] + before[1][k])
            for p in range(len(pieces) // 2):
                pack_s[p * channels : (p + 1) * channels] = jnp.concatenate(
                    pieces[2 * p : 2 * p + 2], axis=1
                )
            base = len(pieces) // 2 * channels
            column = jnp.sum(jnp.transpose(gb_s[...]), axis=0, keepdims=True)
            pack_s[base:] = jnp.zeros((packed - base, 2 * channels), F32)
            pack_s[base : base + 1, 0:channels] = column
            mine_ref, other_ref = results
            at = side_ref[0]
            mine_ref[...] = pack_s[pl.ds(pl.multiple_of(at * half, 8), half)]
            other_ref[...] = pack_s[pl.ds(pl.multiple_of((1 - at) * half, 8), half)]
        else:
            gs_ref, gt_ref, gb_ref = results
            gs_ref[...] = gs_s[...]
            for k in range(taps):
                gt_ref[k] = temporal[k]
            gb_ref[...] = gb_s[...]

    view = (owners, local) + cotangent.shape[-2:]
    operands = [
        lines,
        cotangent.reshape(view),
        back_grad.reshape(view),
        weights,
        bias_tile,
    ]
    in_specs = [ON_CHIP] * len(operands)
    if not final:
        operands[1] = pltpu.with_memory_space_constraint(operands[1], pltpu.HBM)
        in_specs[1] = IN_HBM
        scratch_last = [pltpu.SemaphoreType.DMA(())]
    else:
        scratch_last = []
    shapes = [jax.ShapeDtypeStruct((owners, local, channels, pixels), BF16)]
    square = (trio, trio)
    slab = (taps, channels, channels)
    tile = (channels, cols)
    scratch = [
        pltpu.VMEM((trio, per * local * pixels), BF16),
        pltpu.VMEM((ahead * channels, near_frames * channels), F32),
        pltpu.VMEM(square, F32),
        pltpu.VMEM(tile, F32),
    ]
    scratch += scratch_last
    if halo is not None:
        operands = list(halo) + operands
        in_specs = [SCALARS, ON_CHIP, ON_CHIP] + in_specs
        scratch += [pltpu.VMEM((owners, members, local, width, cols), BF16)] * 2
    if final:
        operands += list(sums)
        in_specs += [ON_CHIP] * 3
        shapes += [jax.ShapeDtypeStruct((half, 2 * channels), F32)] * 2
        scratch += [pltpu.VMEM((packed, 2 * channels), F32)]
    else:
        shapes += [jax.ShapeDtypeStruct(s, F32) for s in (square, slab, tile)]
        shapes += [jax.ShapeDtypeStruct(view, BF16)]
    hidden, *rest = call(
        kernel,
        name,
        tuple(shapes),
        8 * (2 * 9 + taps) * channels * total * channels * pixels,
        scratch=scratch,
        in_specs=in_specs,
        out_specs=tuple(ON_CHIP for _ in shapes),
    )(*operands)
    return [hidden.reshape(total, channels, pixels)] + rest


def sum_over_devices(mine, other, owners, beside, beneath):
    part = mine + lax.ppermute(other, BOTH, beside)
    bits = [1 << n for n in range(owners.bit_length() - 1)]
    orders = (bits, bits[1:] + bits[:1])
    for stage in range(len(bits)):
        pairs = [
            (2 * f + c, 2 * (f ^ orders[c][stage]) + c) for f in range(owners) for c in range(2)
        ]
        part = part + lax.ppermute(part, BOTH, pairs)
        if beneath:
            part = beneath.pop(0)(part)
    return part


def unpack(side, mine, other, taps, channels):
    half = mine.shape[0]

    def kernel(side_ref, mine_ref, other_ref, gs_ref, gb_ref, gt_ref, pack_s):
        at = side_ref[0]
        pack_s[pl.ds(pl.multiple_of(at * half, 8), half)] = mine_ref[...]
        pack_s[pl.ds(pl.multiple_of((1 - at) * half, 8), half)] = other_ref[...]
        for n in range(9 + taps):
            p, u = n // 2, n % 2
            piece = pack_s[p * channels : (p + 1) * channels, u * channels : (u + 1) * channels]
            if n < 9:
                gs_ref[n] = piece
            else:
                gt_ref[n - 9] = piece
        base = (9 + taps) // 2 * channels
        gb_ref[...] = pack_s[base : base + 1, 0:channels]

    return call(
        kernel,
        "unpack",
        (
            jax.ShapeDtypeStruct((9, channels, channels), F32),
            jax.ShapeDtypeStruct((1, channels), F32),
            jax.ShapeDtypeStruct((taps, channels, channels), F32),
        ),
        mine.size,
        scratch=[pltpu.VMEM((2 * half, 2 * channels), F32)],
        in_specs=[SCALARS, ON_CHIP, ON_CHIP],
    )(side, mine, other)


def make_body(owners, members):
    count = owners * members
    beside = [(i, i ^ 1) for i in range(count)]
    beyond = [(i, i - 1) for i in range(2, count, 2)] + [(i, i + 1) for i in range(1, count - 1, 2)]

    def body(frames, spatial_weight, spatial_bias, temporal_weight, cotangent):
        channels = spatial_weight.shape[1]
        taps = temporal_weight.shape[0]
        cols = frames.shape[3]
        side = lax.axis_index("chan").astype(jnp.int32).reshape(1)
        lines = lax.all_to_all(pack(frames, count), BOTH, split_axis=0, concat_axis=0, tiled=True)
        lines = lines.reshape((owners, members) + lines.shape[1:])
        rows = lines.shape[3]
        back_grad, weights, bias_tile = prepare(
            cotangent, temporal_weight, spatial_weight, spatial_bias.reshape(1, channels), cols
        )
        near_row, far_row = edge_rows(side, lines)
        far = lax.ppermute(far_row, BOTH, beyond)
        near = lax.ppermute(near_row, BOTH, beside)
        shared = (back_grad, weights, bias_tile, taps)
        inside = list(range(1, rows - 1))
        inner, *sums, cot = layer(
            "layer_inside", inside, lines, None, cotangent, *shared, None, INSIDE_FRAMES
        )
        halo = (side, near, far)
        outer, mine, other = layer(
            "layer_edges", [0, rows - 1], lines, halo, cot, *shared, sums, EDGE_FRAMES
        )
        made = []

        def output_of(parity):
            def step(part):
                value = temporal_output(inner, outer, temporal_weight, parity, *made)
                part, value = lax.optimization_barrier((part, value))
                made[:] = [value]
                return part

            return step

        part = sum_over_devices(mine, other, owners, beside, [output_of(0), output_of(1)])
        rest = lax.ppermute(part, BOTH, beside)
        grad_spatial, grad_bias, grad_temporal = unpack(side, part, rest, taps, channels)
        return (
            made[0].reshape(cotangent.shape),
            grad_spatial,
            grad_bias.reshape(channels),
            grad_temporal,
        )

    return body


def solution(mesh):
    return jax.shard_map(
        make_body(mesh.shape["frame"], mesh.shape["chan"]),
        mesh=mesh,
        in_specs=(
            P(("groups", "frame"), "chan", None, None),
            P(),
            P(),
            P(),
            P("groups", None, ("frame", "chan")),
        ),
        out_specs=(
            P("groups", None, ("frame", "chan")),
            P("groups", None, None),
            P("groups"),
            P("groups", None, None),
        ),
        check_vma=False,
    )
```

```python
import math

import jax
import jax.numpy as jnp
from jax import lax
from jax.experimental import pallas as pl
from jax.experimental.pallas import tpu as pltpu
from jax.sharding import PartitionSpec as P

FRAME_DILATION = 2
INSIDE_FRAMES = 8
EDGE_FRAMES = 8
PACK_ROWS = 16
BOTH = ("frame", "chan")
F32 = jnp.float32
BF16 = jnp.bfloat16
LANES_IN_LANES = (((1,), (1,)), ((), ()))


def call(
    kernel, name, out_shape, flops, scratch=(), grid=None, in_specs=None, out_specs=None, **more
):
    shapes = out_shape if isinstance(out_shape, tuple) else (out_shape,)
    nbytes = sum(2 * math.prod(s.shape) * jnp.dtype(s.dtype).itemsize for s in shapes)
    cost = pl.CostEstimate(flops=flops, transcendentals=0, bytes_accessed=nbytes)
    params = dict(out_shape=out_shape, scratch_shapes=list(scratch), name=name, **more)
    params.update(cost_estimate=cost)
    if grid is not None:
        params.update(grid=grid)
    if in_specs is not None:
        params.update(in_specs=in_specs)
    if out_specs is not None:
        params.update(out_specs=out_specs)
    return pl.pallas_call(
        kernel, compiler_params=pltpu.CompilerParams(vmem_limit_bytes=24 << 20), **params
    )


IN_HBM = pl.BlockSpec(memory_space=pltpu.HBM)
ON_CHIP = pl.BlockSpec(memory_space=pltpu.VMEM)
SCALARS = pl.BlockSpec(memory_space=pltpu.SMEM)


def pack(frames, blocks):
    local, width, height, cols = frames.shape
    rows = height // blocks
    tile = PACK_ROWS
    per = tile // rows
    shape = (blocks, local, rows, width, cols)

    def kernel(images_ref, out_ref, images_s, lines_s, in_sems, out_sems):
        def fetch(i):
            part = pl.ds(i * tile, tile)
            return pltpu.make_async_copy(
                images_ref.at[:, :, part], images_s.at[:, :, part], in_sems.at[i]
            )

        def ship(i):
            part = pl.ds(i * per, per)
            return pltpu.make_async_copy(lines_s.at[part], out_ref.at[part], out_sems.at[i])

        steps = range(height // tile)
        for i in steps:
            fetch(i).start()
        for i in steps:
            fetch(i).wait()
            for j in range(local):
                lines = jnp.swapaxes(images_s[j, :, i * tile : (i + 1) * tile], 0, 1)
                for d in range(per):
                    lines_s[i * per + d, j] = lines[d * rows : (d + 1) * rows]
            ship(i).start()
        for i in steps:
            ship(i).wait()

    return call(
        kernel,
        "pack",
        pltpu.HBM(shape, frames.dtype),
        frames.size,
        scratch=[
            pltpu.VMEM(frames.shape, frames.dtype),
            pltpu.VMEM(shape, frames.dtype),
            pltpu.SemaphoreType.DMA((height // tile,)),
            pltpu.SemaphoreType.DMA((height // tile,)),
        ],
        in_specs=[IN_HBM],
        out_specs=IN_HBM,
    )(pltpu.with_memory_space_constraint(frames, pltpu.HBM))


def edge_rows(side, lines):
    owners, members, local, rows, width, cols = lines.shape
    shape = jax.ShapeDtypeStruct((owners, members, local, width, cols), lines.dtype)

    def kernel(side_ref, lines_ref, near_ref, far_ref):
        @pl.when(side_ref[0] == 0)
        def _():
            near_ref[...] = lines_ref[:, :, :, rows - 1]
            far_ref[...] = lines_ref[:, :, :, 0]

        @pl.when(side_ref[0] == 1)
        def _():
            near_ref[...] = lines_ref[:, :, :, 0]
            far_ref[...] = lines_ref[:, :, :, rows - 1]

    return call(
        kernel,
        "edge_rows",
        (shape, shape),
        lines.size,
        in_specs=[SCALARS, ON_CHIP],
        out_specs=(ON_CHIP, ON_CHIP),
    )(side, lines)


def prepare(cotangent, temporal_weight, spatial_weight, bias, cols):
    total, channels, pixels = cotangent.shape
    taps = temporal_weight.shape[0]
    lag = FRAME_DILATION
    span = min(pixels, 256)

    def kernel(cot_ref, tw_ref, sw_ref, bias_ref, out_ref, w_ref, tile_ref, ahead_s):
        @pl.when(pl.program_id(0) == 0)
        def _():
            for k in range(taps):
                turned = jnp.transpose(tw_ref[k].astype(F32))
                ahead_s[:, k * channels : (k + 1) * channels] = turned.astype(BF16)
            for q in range(3):
                for s in range(3):
                    w_ref[s * channels : (s + 1) * channels, q * channels : (q + 1) * channels] = (
                        sw_ref[3 * q + s]
                    )
            tile_ref[...] = jnp.transpose(jnp.broadcast_to(bias_ref[...], (cols, channels)))

        for t in range(total):
            here = [k for k in range(taps) if t + k * lag < total]
            weights = ahead_s[:, : len(here) * channels]
            ahead = jnp.concatenate([cot_ref[t + k * lag] for k in here], axis=0)
            grad = jnp.dot(weights, ahead, preferred_element_type=F32)
            out_ref[t] = (grad + cot_ref[t].astype(F32)).astype(BF16)

    def fixed(shape):
        return pl.BlockSpec(shape, lambda n: (0,) * len(shape))

    trio = (3 * channels, 3 * channels)
    part = pl.BlockSpec((total, channels, span), lambda n: (0, 0, n))
    return call(
        kernel,
        "prepare",
        (
            pltpu.HBM(cotangent.shape, BF16),
            jax.ShapeDtypeStruct(trio, BF16),
            jax.ShapeDtypeStruct((channels, cols), F32),
        ),
        8 * taps * channels * cotangent.size,
        scratch=[pltpu.VMEM((channels, taps * channels), BF16)],
        grid=(pixels // span,),
        in_specs=[
            part,
            fixed(temporal_weight.shape),
            fixed(spatial_weight.shape),
            fixed(bias.shape),
        ],
        out_specs=(
            part,
            fixed(trio),
            fixed((channels, cols)),
        ),
    )(
        pltpu.with_memory_space_constraint(cotangent, pltpu.HBM),
        temporal_weight,
        spatial_weight,
        bias,
    )


def temporal_output(inner, outer, temporal_weight, parity, rest=None):
    total, channels, inside = inner.shape
    span = outer.shape[2]
    cols = span // 2
    count = total // 2
    pixels = inside + span
    taps = temporal_weight.shape[0]

    def kernel(*refs):
        inner_ref, outer_ref, tw_ref, out_ref, w_s = refs[0], refs[1], refs[2], refs[-2], refs[-1]
        for k in range(taps):
            w_s[:, k * channels : (k + 1) * channels] = tw_ref[k]
        for f in range(count):
            here = [k for k in range(taps) if f - k >= 0]
            weights = w_s[:, : len(here) * channels]

            def value_of(ref, at):
                delayed = jnp.concatenate(
                    [ref[f - k, 0, :, at : at + span] for k in here], axis=0
                )
                value = jnp.dot(weights, delayed, preferred_element_type=F32)
                return (value + ref[f, 0, :, at : at + span].astype(F32)).astype(BF16)

            for at in range(0, inside, span):
                out_ref[f, 0, :, cols + at : cols + at + span] = value_of(inner_ref, at)
            value = value_of(outer_ref, 0)
            out_ref[f, 0, :, :cols] = value[:, :cols]
            out_ref[f, 0, :, pixels - cols :] = value[:, cols:]

    def part(width):
        return pl.BlockSpec((count, 1, channels, width), lambda i: (0, parity, 0, 0))

    in_specs = [
        part(inside),
        part(span),
        pl.BlockSpec(temporal_weight.shape, lambda i: (0, 0, 0)),
    ]
    operands = [
        inner.reshape(count, 2, channels, inside),
        outer.reshape(count, 2, channels, span),
        temporal_weight,
    ]
    more = {}
    if rest is not None:
        in_specs.append(pl.BlockSpec(memory_space=pl.ANY))
        operands.append(rest)
        more["input_output_aliases"] = {3: 0}
    return call(
        kernel,
        "temporal_output",
        jax.ShapeDtypeStruct((count, 2, channels, pixels), BF16),
        8 * taps * channels * inner.size,
        scratch=[pltpu.VMEM((channels, taps * channels), BF16)],
        grid=(1,),
        in_specs=in_specs,
        out_specs=part(pixels),
        **more,
    )(*operands)


def gelu_and_slope(values):
    scale = 0.7978845608
    cubic = (scale * 0.044715) * (values * values)
    bent = jnp.tanh(values * (scale + cubic))
    half = 0.5 + 0.5 * bent
    active = values * half
    slope = half * (1.0 + (values - active) * (2.0 * scale + 6.0 * cubic))
    return active, slope


def layer(name, listed, lines, halo, cotangent, back_grad, weights, bias_tile, taps, sums, per):
    owners, members, local, rows, width, cols = lines.shape
    total = owners * local
    channels = members * width
    pixels = len(listed) * cols
    final = sums is not None
    packed = (9 + taps + 1) // 2 * channels + 16
    half = packed // 2
    trio = 3 * channels
    joined = local if pixels <= 512 else 1
    near_frames = 4
    ahead = near_frames + taps - 1
    pieces_of = []
    for at, r in enumerate(listed):
        if pieces_of and pieces_of[-1][0] + pieces_of[-1][2] == r:
            pieces_of[-1][2] += 1
        else:
            pieces_of.append([r, at, 1])
    def kernel(*refs):
        refs = list(refs)
        if halo is not None:
            side_ref, near_ref, far_ref = refs[:3]
            refs = refs[3:]
        x_ref, cot_ref, back_ref, w_ref, bias_ref = refs[:5]
        refs = refs[5:]
        if final:
            before = refs[:3]
            refs = refs[3:]
        hid_ref = refs.pop(0)
        results = refs[: 2 if final else 4]
        refs = refs[2 if final else 4 :]
        gp_s, pair_s, gs_s, gb_s = refs[:4]
        refs = refs[4:]
        if final:
            cot_s = cot_ref
        else:
            cot_s, cot_sem = results.pop(), refs.pop(0)
        if not final:
            cot_copy = pltpu.make_async_copy(cot_ref, cot_s, cot_sem)
            cot_copy.start()

        if halo is not None:
            top_s, bottom_s = refs[:2]
            refs = refs[2:]

            @pl.when(side_ref[0] == 0)
            def _():
                top_s[...] = far_ref[...]
                bottom_s[...] = near_ref[...]

            @pl.when(side_ref[0] == 1)
            def _():
                top_s[...] = near_ref[...]
                bottom_s[...] = far_ref[...]

        lane = lax.broadcasted_iota(jnp.int32, (channels, cols), 1)
        first = lane == 0
        last = lane == cols - 1

        def shifted(tile, by):
            if by == 1:
                return jnp.where(first, 0.0, pltpu.roll(tile, 1, 1))
            return jnp.where(last, 0.0, pltpu.roll(tile, cols - 1, 1))

        def row(f, j, r):
            if r < 0:
                return [top_s[f, c, j] for c in range(members)]
            if r == rows:
                return [bottom_s[f, c, j] for c in range(members)]
            return [x_ref[f, c, j, r] for c in range(members)]

        def three_rows(f, j, r):
            return jnp.concatenate(row(f, j, r - 1) + row(f, j, r) + row(f, j, r + 1), axis=0)

        if final:
            gs_s[...] = before[0][...]
            gb_s[...] = before[2][...]
        else:
            gs_s[...] = jnp.zeros_like(gs_s)
            gb_s[...] = jnp.zeros_like(gb_s)

        def some_frames(i, carry):
            bias_sum = None
            for p in range(per):
                f = i * per + p
                for j0 in range(0, local, joined):
                    sources = [
                        (j, n, r) for j in range(j0, j0 + joined) for n, r in enumerate(listed)
                    ]
                    stack = jnp.concatenate([three_rows(f, j, r) for j, n, r in sources], axis=1)
                    conv = jnp.dot(w_ref[...], stack, preferred_element_type=F32)
                    for u, (j, n, r) in enumerate(sources):
                        lo = u * cols
                        span = slice(n * cols, n * cols + cols)
                        at = (p * local + j) * pixels + n * cols
                        place = slice(at, at + cols)
                        pre = (
                            shifted(conv[:channels, lo : lo + cols], 1)
                            + conv[channels : 2 * channels, lo : lo + cols]
                            + shifted(conv[2 * channels :, lo : lo + cols], -1)
                            + bias_ref[...]
                        )
                        active, slope = gelu_and_slope(pre)
                        hid_ref[f, j, :, span] = active.astype(BF16)
                        back = back_ref[f, j, :, r * cols : (r + 1) * cols].astype(F32)
                        rounded = (back * slope).astype(BF16)
                        grad = rounded.astype(F32)
                        bias_sum = grad if bias_sum is None else bias_sum + grad
                        nothing = jnp.zeros_like(rounded)
                        gp_s[0:channels, place] = jnp.where(
                            last, nothing, pltpu.roll(rounded, cols - 1, 1)
                        )
                        gp_s[channels : 2 * channels, place] = rounded
                        gp_s[2 * channels :, place] = jnp.where(
                            first, nothing, pltpu.roll(rounded, 1, 1)
                        )
            gb_s[...] += bias_sum
            whole = jnp.concatenate(
                [
                    three_rows(i * per + p, j, r)
                    for p in range(per)
                    for j in range(local)
                    for r in listed
                ],
                axis=1,
            )
            gs_s[...] += lax.dot_general(
                gp_s[...], whole, LANES_IN_LANES, preferred_element_type=F32
            )
            return carry

        lax.fori_loop(0, owners // per, some_frames, 0)

        if not final:
            cot_copy.wait()

        def reached(f, count, j):
            parts = [
                cot_s[f : f + count, j, :, start * cols : (start + length) * cols]
                for start, at, length in pieces_of
            ]
            joint = parts[0] if len(parts) == 1 else jnp.concatenate(parts, axis=2)
            return joint.reshape(count * channels, pixels)

        for f in range(0, owners, near_frames):
            count = min(ahead, owners - f)
            reach = jnp.concatenate([reached(f, count, j) for j in range(local)], axis=1)
            delayed = jnp.concatenate(
                [
                    hid_ref[f : f + near_frames, j].reshape(near_frames * channels, pixels)
                    for j in range(local)
                ],
                axis=1,
            )
            pairs = lax.dot_general(
                reach, delayed, LANES_IN_LANES, preferred_element_type=F32
            )
            if f > 0:
                pair_s[0 : count * channels] += pairs
            else:
                pair_s[0 : count * channels] = pairs
                if count < ahead:
                    pair_s[count * channels :] = jnp.zeros_like(pair_s[count * channels :])
        temporal = []
        for k in range(taps):
            block = None
            for a in range(near_frames):
                more = pair_s[
                    (a + k) * channels : (a + k + 1) * channels, a * channels : (a + 1) * channels
                ]
                block = more if block is None else block + more
            temporal.append(block)

        if final:
            (pack_s,) = refs
            pieces = []
            for q in range(3):
                for s in range(3):
                    pieces.append(
                        gs_s[s * channels : (s + 1) * channels, q * channels : (q + 1) * channels]
                    )
            for k in range(taps):
                pieces.append(temporal[k] + before[1][k])
            for p in range(len(pieces) // 2):
                pack_s[p * channels : (p + 1) * channels] = jnp.concatenate(
                    pieces[2 * p : 2 * p + 2], axis=1
                )
            base = len(pieces) // 2 * channels
            column = jnp.sum(jnp.transpose(gb_s[...]), axis=0, keepdims=True)
            pack_s[base:] = jnp.zeros((packed - base, 2 * channels), F32)
            pack_s[base : base + 1, 0:channels] = column
            mine_ref, other_ref = results
            at = side_ref[0]
            mine_ref[...] = pack_s[pl.ds(pl.multiple_of(at * half, 8), half)]
            other_ref[...] = pack_s[pl.ds(pl.multiple_of((1 - at) * half, 8), half)]
        else:
            gs_ref, gt_ref, gb_ref = results
            gs_ref[...] = gs_s[...]
            for k in range(taps):
                gt_ref[k] = temporal[k]
            gb_ref[...] = gb_s[...]

    view = (owners, local) + cotangent.shape[-2:]
    operands = [
        lines,
        cotangent.reshape(view),
        back_grad.reshape(view),
        weights,
        bias_tile,
    ]
    in_specs = [ON_CHIP] * len(operands)
    if not final:
        operands[1] = pltpu.with_memory_space_constraint(operands[1], pltpu.HBM)
        in_specs[1] = IN_HBM
        scratch_last = [pltpu.SemaphoreType.DMA(())]
    else:
        scratch_last = []
    shapes = [jax.ShapeDtypeStruct((owners, local, channels, pixels), BF16)]
    square = (trio, trio)
    slab = (taps, channels, channels)
    tile = (channels, cols)
    scratch = [
        pltpu.VMEM((trio, per * local * pixels), BF16),
        pltpu.VMEM((ahead * channels, near_frames * channels), F32),
        pltpu.VMEM(square, F32),
        pltpu.VMEM(tile, F32),
    ]
    scratch += scratch_last
    if halo is not None:
        operands = list(halo) + operands
        in_specs = [SCALARS, ON_CHIP, ON_CHIP] + in_specs
        scratch += [pltpu.VMEM((owners, members, local, width, cols), BF16)] * 2
    if final:
        operands += list(sums)
        in_specs += [ON_CHIP] * 3
        shapes += [jax.ShapeDtypeStruct((half, 2 * channels), F32)] * 2
        scratch += [pltpu.VMEM((packed, 2 * channels), F32)]
    else:
        shapes += [jax.ShapeDtypeStruct(s, F32) for s in (square, slab, tile)]
        shapes += [jax.ShapeDtypeStruct(view, BF16)]
    hidden, *rest = call(
        kernel,
        name,
        tuple(shapes),
        8 * (2 * 9 + taps) * channels * total * channels * pixels,
        scratch=scratch,
        in_specs=in_specs,
        out_specs=tuple(ON_CHIP for _ in shapes),
    )(*operands)
    return [hidden.reshape(total, channels, pixels)] + rest


def sum_over_devices(mine, other, owners, beside, beneath):
    part = mine + lax.ppermute(other, BOTH, beside)
    bits = [1 << n for n in range(owners.bit_length() - 1)]
    orders = (bits, bits[1:] + bits[:1])
    for stage in range(len(bits)):
        pairs = [
            (2 * f + c, 2 * (f ^ orders[c][stage]) + c) for f in range(owners) for c in range(2)
        ]
        part = part + lax.ppermute(part, BOTH, pairs)
        if stage > 0 and beneath:
            part = beneath.pop(0)(part)
    return part


def unpack(side, mine, other, taps, channels):
    half = mine.shape[0]

    def kernel(side_ref, mine_ref, other_ref, gs_ref, gb_ref, gt_ref, pack_s):
        at = side_ref[0]
        pack_s[pl.ds(pl.multiple_of(at * half, 8), half)] = mine_ref[...]
        pack_s[pl.ds(pl.multiple_of((1 - at) * half, 8), half)] = other_ref[...]
        for n in range(9 + taps):
            p, u = n // 2, n % 2
            piece = pack_s[p * channels : (p + 1) * channels, u * channels : (u + 1) * channels]
            if n < 9:
                gs_ref[n] = piece
            else:
                gt_ref[n - 9] = piece
        base = (9 + taps) // 2 * channels
        gb_ref[...] = pack_s[base : base + 1, 0:channels]

    return call(
        kernel,
        "unpack",
        (
            jax.ShapeDtypeStruct((9, channels, channels), F32),
            jax.ShapeDtypeStruct((1, channels), F32),
            jax.ShapeDtypeStruct((taps, channels, channels), F32),
        ),
        mine.size,
        scratch=[pltpu.VMEM((2 * half, 2 * channels), F32)],
        in_specs=[SCALARS, ON_CHIP, ON_CHIP],
    )(side, mine, other)


def make_body(owners, members):
    count = owners * members
    beside = [(i, i ^ 1) for i in range(count)]
    beyond = [(i, i - 1) for i in range(2, count, 2)] + [(i, i + 1) for i in range(1, count - 1, 2)]

    def body(frames, spatial_weight, spatial_bias, temporal_weight, cotangent):
        channels = spatial_weight.shape[1]
        taps = temporal_weight.shape[0]
        cols = frames.shape[3]
        side = lax.axis_index("chan").astype(jnp.int32).reshape(1)
        lines = lax.all_to_all(pack(frames, count), BOTH, split_axis=0, concat_axis=0, tiled=True)
        lines = lines.reshape((owners, members) + lines.shape[1:])
        rows = lines.shape[3]
        back_grad, weights, bias_tile = prepare(
            cotangent, temporal_weight, spatial_weight, spatial_bias.reshape(1, channels), cols
        )
        near_row, far_row = edge_rows(side, lines)
        far = lax.ppermute(far_row, BOTH, beyond)
        near = lax.ppermute(near_row, BOTH, beside)
        shared = (back_grad, weights, bias_tile, taps)
        inside = list(range(1, rows - 1))
        inner, *sums, cot = layer(
            "layer_inside", inside, lines, None, cotangent, *shared, None, INSIDE_FRAMES
        )
        halo = (side, near, far)
        outer, mine, other = layer(
            "layer_edges", [0, rows - 1], lines, halo, cot, *shared, sums, EDGE_FRAMES
        )
        made = []

        def output_of(parity):
            def step(part):
                value = temporal_output(inner, outer, temporal_weight, parity, *made)
                part, value = lax.optimization_barrier((part, value))
                made[:] = [value]
                return part

            return step

        part = sum_over_devices(mine, other, owners, beside, [output_of(0), output_of(1)])
        rest = lax.ppermute(part, BOTH, beside)
        grad_spatial, grad_bias, grad_temporal = unpack(side, part, rest, taps, channels)
        return (
            made[0].reshape(cotangent.shape),
            grad_spatial,
            grad_bias.reshape(channels),
            grad_temporal,
        )

    return body


def solution(mesh):
    return jax.shard_map(
        make_body(mesh.shape["frame"], mesh.shape["chan"]),
        mesh=mesh,
        in_specs=(
            P(("groups", "frame"), "chan", None, None),
            P(),
            P(),
            P(),
            P("groups", None, ("frame", "chan")),
        ),
        out_specs=(
            P("groups", None, ("frame", "chan")),
            P("groups", None, None),
            P("groups"),
            P("groups", None, None),
        ),
        check_vma=False,
    )
```
